32 devices in a mesh: rep: 2 (over y), ctx: 4 (over z), ch: 2 (over x), sub: 2 (over core).
Axes of the slice: x: 2, y: 2, z: 4, core: 2. Of those that a mesh axis runs over, the one named last changes fastest.
Arguments:
- hyena_query: bfloat16 [3072, 8192], P(('rep', 'ctx'), ('ch', 'sub')), parts along dimension 0, may hold values from -6 to 6
- hyena_key: bfloat16 [3072, 8192], P(('rep', 'ctx'), ('ch', 'sub')), parts along dimension 0, may hold values from -6 to 6
- hyena_value: bfloat16 [3072, 8192], P(('rep', 'ctx'), ('ch', 'sub')), parts along dimension 0, may hold values from -6 to 6
- filters: bfloat16 [512, 128], P(('ch', 'sub')), may hold values from -0.5 to 0.5
- skip_gain: float32 [8192], P(('ch', 'sub')), may hold values from 0.5 to 1.5
- attn_query: bfloat16 [3072, 8192], P(('rep', 'ctx'), ('ch', 'sub')), parts along dimension 0, may hold values from -40 to 40
- attn_key: bfloat16 [3072, 8192], P(('rep', 'ctx'), ('ch', 'sub')), parts along dimension 0, may hold values from -5 to 5
- genome_starts: int32 [8], P('rep'), parts along dimension 0, may hold values from 0 to 1408, as said below
Outputs:
- hyena_mix: bfloat16 [3072, 8192], P(('rep', 'ctx'), ('ch', 'sub')), parts along dimension 0
- attended: bfloat16 [3072, 8192], P(('rep', 'ctx'), ('ch', 'sub')), parts along dimension 0
The draws below stay inside these ranges and needn't reach their ends.
There are 2 independent parts, one for each index of `rep`. The reference program is written for one: setup_inputs(seed, part) draws one part's arguments, and reference() takes and returns one part's arrays. A program takes and returns all parts, laid end to end along the dimension named above; an argument that names none is the same for every part. Nothing has to cross between parts.
Inputs may be any that keep to these rules, and one draw needn't show every extreme that they name: genome_starts[0] is 0; the entries rise, each by 128 or more, and the last genome holds exactly 128 positions.
All inputs are finite; a program needn't handle non-finite values.
Results may differ from the reference program's by a relative error of at most 0.0059.
Values may be sent and summed in bfloat16 or wider, within the bound.
A program may use at most 128 MiB of HBM per device.

```python
import math
import jax
import jax.numpy as jnp
from jax import lax

D = 8192
HEAD_DIM = 128
FILTER = 128
GROUP = 16
GENOMES = 4
TOKENS = 1536


def shared_keys(key):
    return jnp.clip(jax.random.normal(jax.random.fold_in(key, 101), (TOKENS, D), jnp.float32), -4.0, 4.0)


def draw_attn_key(key, part):
    return shared_keys(key).astype(jnp.bfloat16)


def draw_attn_query(key, part):
    drawn = 2.0 * jax.random.normal(jax.random.fold_in(key, 201), (TOKENS, D), jnp.float32)
    return jnp.clip(drawn, -8.0, 8.0).astype(jnp.bfloat16)


def draw_genome_starts(key, part):
    cuts = jax.random.randint(jax.random.fold_in(key, 301), (GENOMES - 2,), 0, TOKENS - GENOMES * FILTER + 1, dtype=jnp.int32)
    ordered = jnp.sort(cuts) + FILTER * jnp.arange(1, GENOMES - 1, dtype=jnp.int32)
    last = jnp.full((1,), TOKENS - FILTER, jnp.int32)
    return jnp.concatenate([jnp.zeros((1,), jnp.int32), ordered.astype(jnp.int32), last])


def steps_of(rng, shape, split, smallest, largest):
    loudness, own = 1.0, jax.random.fold_in(rng, 6)
    for dim, blocks in split:
        steps = jnp.exp(jax.random.uniform(jax.random.fold_in(own, dim), (blocks,), jnp.float32, smallest / len(split), largest / len(split)))
        loudness = loudness * jnp.repeat(steps, shape[dim] // blocks).reshape([-1 if axis == dim else 1 for axis in range(len(shape))])
    return loudness


def scatter_about(key, shape, spread, most, shards=(), held_as=jnp.bfloat16):
    values = spread * jax.random.normal(key, shape, jnp.float32)
    if shards:
        values = values * steps_of(key, shape, shards, -0.22, 0.18)
    return jnp.clip(values, -most, most).astype(held_as)


def setup_inputs(seed: int = 0, part: int = 0) -> dict:
    seeds = jax.random.split(jax.random.key(seed), 9)
    part_splits = jax.random.split(jax.random.fold_in(seeds[8], part), 9)
    return {
        "hyena_query": scatter_about(part_splits[0], (TOKENS, D), 1.0, 6.0, ((0, 4), (1, 4))),
        "hyena_key": scatter_about(part_splits[1], (TOKENS, D), 1.0, 6.0, ((0, 4), (1, 4))),
        "hyena_value": scatter_about(part_splits[2], (TOKENS, D), 1.0, 6.0, ((0, 4), (1, 4))),
        "filters": scatter_about(seeds[3], (D // GROUP, FILTER), FILTER ** -0.5, 0.5, ((0, 4),)),
        "skip_gain": jnp.clip(0.5 + 1.0 * jax.random.uniform(seeds[4], (D,), jnp.float32) ** steps_of(seeds[4], (D,), ((0, 4),), -0.2, 0.2), 0.5, 1.5),
        "attn_query": draw_attn_query(jax.random.fold_in(jax.random.fold_in(seeds[8], part), 71), part),
        "attn_key": draw_attn_key(jax.random.fold_in(jax.random.fold_in(seeds[8], part), 71), part),
        "genome_starts": draw_genome_starts(jax.random.fold_in(jax.random.fold_in(seeds[8], part), 71), part),
    }


def genome_begin(positions, genome_starts):
    inside = genome_starts[None, :] <= positions[:, None]
    return lax.optimization_barrier(jnp.max(jnp.where(inside, genome_starts[None, :], 0), axis=1))

def reference(hyena_query, hyena_key, hyena_value, filters, skip_gain, attn_query, attn_key, genome_starts):
    product = lax.optimization_barrier((hyena_key.astype(jnp.float32) * hyena_value.astype(jnp.float32)).astype(jnp.bfloat16))
    positions = jnp.arange(TOKENS, dtype=jnp.int32)
    begins = genome_begin(positions, genome_starts)
    product_wide = product.astype(jnp.float32)
    padded = jnp.concatenate([jnp.zeros((FILTER - 1, D), jnp.float32), product_wide], axis=0)
    filters_wide = filters.astype(jnp.float32)

    def one_tap(total, tap):
        start = (FILTER - 1 - tap).astype(jnp.int32)
        shifted = lax.dynamic_slice_in_dim(padded, start, TOKENS, 0)
        column = lax.dynamic_slice_in_dim(filters_wide, tap.astype(jnp.int32), 1, 1)[:, 0]
        gains = jnp.repeat(column, GROUP)
        valid = positions - tap >= begins
        return (total + jnp.where(valid[:, None], shifted * gains[None, :], jnp.zeros((), jnp.float32)), None)
    filtered, unused = lax.scan(one_tap, jnp.zeros((TOKENS, D), jnp.float32), jnp.arange(FILTER, dtype=jnp.int32))
    hyena_mix = (hyena_query.astype(jnp.float32) * (filtered + skip_gain[None, :] * product_wide)).astype(jnp.bfloat16)
    score_scale = 1.0 / math.sqrt(HEAD_DIM)
    head_count = D // HEAD_DIM
    block = math.gcd(TOKENS, 512)
    blocks = TOKENS // block
    query_heads = attn_query.reshape(TOKENS, head_count, HEAD_DIM).transpose(1, 0, 2)
    key_heads = attn_key.reshape(TOKENS, head_count, HEAD_DIM).transpose(1, 0, 2)
    value_heads = hyena_mix.reshape(TOKENS, head_count, HEAD_DIM).transpose(1, 0, 2)
    pos_blocks = positions.reshape(blocks, block)
    begin_blocks = begins.reshape(blocks, block)

    def one_head(operands):
        query_head, key_head, value_head = operands

        def one_block(block_ops):
            query_block, query_pos, query_begin = block_ops
            visible = (positions[None, :] <= query_pos[:, None]) & (positions[None, :] >= query_begin[:, None])
            scores = jnp.dot(query_block, key_head.T, preferred_element_type=jnp.float32) * score_scale
            highest = lax.optimization_barrier(jnp.max(jnp.where(visible, scores, -1e+30), axis=1, keepdims=True))
            weights = jnp.exp(jnp.where(visible, scores - highest, -1e+30))
            weight_sum = lax.optimization_barrier(jnp.sum(weights, axis=1, keepdims=True))
            mixed = jnp.dot(weights.astype(jnp.bfloat16), value_head, preferred_element_type=jnp.float32) / weight_sum
            return mixed.astype(jnp.bfloat16)
        pieces = lax.map(one_block, (query_head.reshape(blocks, block, HEAD_DIM), pos_blocks, begin_blocks))
        return pieces.reshape(TOKENS, HEAD_DIM)
    outputs = lax.map(one_head, (query_heads, key_heads, value_heads))
    attended = outputs.transpose(1, 0, 2).reshape(TOKENS, D)
    return (hyena_mix, attended)
```

```python
from functools import partial
import math

import jax
import jax.numpy as jnp
from jax import lax
from jax.experimental import pallas as pl
from jax.experimental.pallas import tpu as pltpu
from jax.sharding import PartitionSpec as P

HEAD_DIM = 128


def passed_along(value, axis, by):
    devices = lax.axis_size(axis)
    pairs = [(i, i + by) for i in range(devices) if 0 <= i + by < devices]
    return lax.ppermute(value, axis, pairs)


def genome_index(positions, genome_starts):
    inside = genome_starts[None, :] <= positions[:, None]
    return jnp.sum(inside.astype(jnp.int32), axis=1) - 1


def genome_begin(positions, genome_starts):
    inside = genome_starts[None, :] <= positions[:, None]
    return jnp.max(jnp.where(inside, genome_starts[None, :], 0), axis=1)


def grouped_filter(product, parity, filters, left_pad):
    channels = product.shape[1]
    group_width = channels // filters.shape[0]
    kernel = jnp.repeat(filters, group_width, axis=0).T[::-1][:, None, :]
    nothing = jnp.zeros_like(product)
    even_rows = jnp.where((parity == 0)[:, None], product, nothing)
    odd_rows = jnp.where((parity == 1)[:, None], product, nothing)
    stacked = jnp.stack([even_rows, odd_rows])
    return lax.conv_general_dilated(
        stacked,
        kernel,
        (1,),
        [(left_pad, 0)],
        dimension_numbers=("NWC", "WIO", "NWC"),
        feature_group_count=channels,
        preferred_element_type=jnp.float32,
    )


def attend_update(carried, queries, query_pos, query_begin, key_heads, value_heads, key_pos):
    weighted, running_max, weight_sum = carried
    score_scale = 1.0 / math.sqrt(HEAD_DIM)
    scores = (
        jnp.einsum("qhd,khd->hqk", queries, key_heads, preferred_element_type=jnp.float32)
        * score_scale
    )
    visible = (key_pos[None, :] <= query_pos[:, None]) & (key_pos[None, :] >= query_begin[:, None])
    new_max = jnp.maximum(running_max, jnp.max(jnp.where(visible[None], scores, -1e30), axis=2))
    weights = jnp.exp(jnp.where(visible[None], scores - new_max[:, :, None], -1e30))
    mixed = jnp.einsum(
        "hqk,khd->hqd",
        weights.astype(jnp.bfloat16),
        value_heads,
        preferred_element_type=jnp.float32,
    )
    return (mixed, new_max, jnp.sum(weights, axis=2))


def keep_state(carried):
    return carried


def gathered_plan(
    hyena_query, hyena_key, hyena_value, filters, skip_gain, attn_query, attn_key, genome_starts
):
    local_rows, channels = hyena_key.shape
    taps = filters.shape[1]
    shard_first = lax.axis_index("ctx") * local_rows
    product = lax.optimization_barrier(
        (hyena_key.astype(jnp.float32) * hyena_value.astype(jnp.float32)).astype(jnp.bfloat16)
    )
    earlier = passed_along(product[local_rows - (taps - 1) :], "ctx", 1)
    extended = jnp.concatenate([earlier, product], axis=0)
    extended_pos = shard_first - (taps - 1) + jnp.arange(local_rows + taps - 1, dtype=jnp.int32)
    both_parities = grouped_filter(
        extended, genome_index(extended_pos, genome_starts) % 2, filters, 0
    )
    own_pos = shard_first + jnp.arange(local_rows, dtype=jnp.int32)
    own_parity = genome_index(own_pos, genome_starts) % 2
    filtered = jnp.where((own_parity == 0)[:, None], both_parities[0], both_parities[1])
    hyena_mix = (
        hyena_query.astype(jnp.float32)
        * (filtered + skip_gain[None, :] * product.astype(jnp.float32))
    ).astype(jnp.bfloat16)
    head_count = channels // HEAD_DIM
    queries = attn_query.reshape(local_rows, head_count, HEAD_DIM)
    pairs = [(queries, own_pos)]
    groups = [
        (group_queries, group_pos, genome_begin(group_pos, genome_starts))
        for group_queries, group_pos in pairs
    ]
    initial = tuple(
        (
            (
                jnp.zeros((head_count, group_pos.shape[0], HEAD_DIM), jnp.float32),
                jnp.full((head_count, group_pos.shape[0]), -1e30, jnp.float32),
                jnp.zeros((head_count, group_pos.shape[0]), jnp.float32),
            )
            for group_queries, group_pos, group_begin in groups
        )
    )
    offset_row = jnp.int32(0)
    keys_piece = lax.all_gather(attn_key, "ctx", axis=0, tiled=True)
    values_piece = lax.all_gather(hyena_mix, "ctx", axis=0, tiled=True)
    key_rows = keys_piece.shape[0]
    key_heads = keys_piece.reshape(key_rows, head_count, HEAD_DIM)
    value_heads = values_piece.reshape(key_rows, head_count, HEAD_DIM)
    key_pos = jnp.arange(key_rows, dtype=jnp.int32)
    updated = []
    for state_now, (group_queries, group_pos, group_begin) in zip(initial, groups):
        needed = (offset_row <= jnp.max(group_pos)) & (offset_row + key_rows > jnp.min(group_begin))
        update = partial(
            attend_update,
            queries=group_queries,
            query_pos=group_pos,
            query_begin=group_begin,
            key_heads=key_heads,
            value_heads=value_heads,
            key_pos=key_pos,
        )
        updated.append(lax.cond(needed, update, keep_state, state_now))
    results = tuple(updated)
    outputs = []
    for weighted, running_max, weight_sum in results:
        finished = (weighted / weight_sum[:, :, None]).astype(jnp.bfloat16)
        outputs.append(finished.transpose(1, 0, 2).reshape(weighted.shape[1], channels))
    attended = outputs[0]
    return (hyena_mix, attended)


NEVER = -1e29
BLOCK = 128
CHUNKS = 4
EXPONENT = math.log2(math.e) / math.sqrt(HEAD_DIM)


def begin_of(positions, facts_ref, genomes):
    begin = jnp.zeros_like(positions)
    for genome in range(genomes):
        start = facts_ref[genome]
        begin = jnp.where(start <= positions, jnp.maximum(begin, start), begin)
    return begin


def hyena_kernel(genomes, facts_ref, query_ref, key_ref, value_ref, halo_ref, taps_ref, gain_ref,
                 mix_ref, extended, masks):
    rows = key_ref.shape[0]
    blocks = rows // BLOCK
    groups = taps_ref.shape[0]
    group_width = BLOCK // groups

    @pl.when(pl.program_id(0) == 0)
    def _():
        first = facts_ref[genomes] * rows
        for b in range(blocks):
            i = lax.broadcasted_iota(jnp.int32, (BLOCK, 2 * BLOCK), 0)
            j = lax.broadcasted_iota(jnp.int32, (BLOCK, 2 * BLOCK), 1) - BLOCK
            begin = begin_of(i + (first + b * BLOCK), facts_ref, genomes)
            tap = i - j
            inside = (tap >= 0) & (tap < BLOCK) & (j + (first + b * BLOCK) >= begin)
            masks[b] = jnp.where(inside, 1.0, 0.0).astype(jnp.bfloat16)

    product = (key_ref[...].astype(jnp.float32) * value_ref[...].astype(jnp.float32)).astype(
        jnp.bfloat16
    )
    extended[:BLOCK] = halo_ref[...]
    extended[BLOCK:] = product
    lane_group = lax.broadcasted_iota(jnp.int32, (BLOCK, BLOCK), 1) // group_width
    totals = [jnp.zeros((BLOCK, BLOCK), jnp.float32) for b in range(blocks)]
    for g in range(groups):
        row = jnp.broadcast_to(taps_ref[g : g + 1, :], (BLOCK, BLOCK))
        turned = pltpu.roll(row, 0, 1, stride=1, stride_axis=0).astype(jnp.bfloat16)
        both = jnp.concatenate([turned, turned], axis=1)
        for b in range(blocks):
            band = both * masks[b]
            part = jnp.dot(
                band, extended[b * BLOCK : (b + 2) * BLOCK], preferred_element_type=jnp.float32
            )
            totals[b] = jnp.where(lane_group == g, part, totals[b])
    for b in range(blocks):
        here = slice(b * BLOCK, (b + 1) * BLOCK)
        wide = extended[(b + 1) * BLOCK : (b + 2) * BLOCK].astype(jnp.float32)
        mix_ref[here] = (
            query_ref[here].astype(jnp.float32) * (totals[b] + gain_ref[...] * wide)
        ).astype(jnp.bfloat16)


def hyena(facts, genomes, query, key, value, halo, turned_taps, skip_gain):
    rows, channels = key.shape
    groups = turned_taps.shape[0] * BLOCK // channels
    column = lambda c, facts_ref: (0, c)
    return pl.pallas_call(
        partial(hyena_kernel, genomes),
        out_shape=jax.ShapeDtypeStruct((rows, channels), jnp.bfloat16),
        grid_spec=pltpu.PrefetchScalarGridSpec(
            num_scalar_prefetch=1,
            grid=(channels // BLOCK,),
            in_specs=[
                pl.BlockSpec((rows, BLOCK), column),
                pl.BlockSpec((rows, BLOCK), column),
                pl.BlockSpec((rows, BLOCK), column),
                pl.BlockSpec((BLOCK, BLOCK), column),
                pl.BlockSpec((groups, BLOCK), lambda c, facts_ref: (c, 0)),
                pl.BlockSpec((1, BLOCK), column),
            ],
            out_specs=pl.BlockSpec((rows, BLOCK), column),
            scratch_shapes=[
                pltpu.VMEM((rows + BLOCK, BLOCK), jnp.bfloat16),
                pltpu.VMEM((rows // BLOCK, BLOCK, 2 * BLOCK), jnp.bfloat16),
            ],
        ),
        cost_estimate=pl.CostEstimate(
            flops=rows * channels * 2 * 2 * BLOCK * groups,
            bytes_accessed=rows * channels * 8,
            transcendentals=0,
        ),
        name="hyena",
    )(facts, query, key, value, halo, turned_taps, skip_gain)


def attend_tile(queries, keys, values, query_first, key_first, facts_ref, genomes, carried):
    scores = lax.dot_general(
        queries, keys, (((1,), (1,)), ((), ())), preferred_element_type=jnp.float32
    )
    query_pos = query_first + lax.broadcasted_iota(jnp.int32, (queries.shape[0], 1), 0)
    begin = begin_of(query_pos, facts_ref, genomes)
    key_pos = key_first + lax.broadcasted_iota(jnp.int32, scores.shape, 1)
    visible = (key_pos >= begin) & (key_pos <= query_pos)
    scores = jnp.where(visible, scores, 10 * NEVER)
    highest, total, mixed = carried
    new_highest = jnp.maximum(highest, jnp.max(scores, axis=1, keepdims=True))
    weights = jnp.exp2((scores - new_highest) * EXPONENT)
    fade = jnp.exp2((highest - new_highest) * EXPONENT)
    new_mixed = fade * mixed + jnp.dot(
        weights.astype(jnp.bfloat16), values, preferred_element_type=jnp.float32
    )
    return new_highest, fade * total + jnp.sum(weights, axis=1, keepdims=True), new_mixed


def attend_kernel(genomes, facts_ref, own_q, next_q, last_q, own_k, own_v, far_k, far_v,
                  own_o, next_o, last_o, own_l, next_l, last_l, high, total, mixed):
    rows = own_q.shape[0]
    head = pl.program_id(0)
    shard = facts_ref[genomes]
    own_first = shard * rows

    def update(here, queries, keys, values, query_first, key_first):
        carried = (high[here], total[here], mixed[here])
        high[here], total[here], mixed[here] = attend_tile(
            queries, keys, values, query_first, key_first, facts_ref, genomes, carried
        )

    def clear():
        high[...] = jnp.full_like(high, NEVER)
        total[...] = jnp.zeros_like(total)
        mixed[...] = jnp.zeros_like(mixed)

    def finish(out_ref, log_ref):
        summed = total[...]
        some = summed > 0
        safe = jnp.where(some, summed, 1.0)
        out_ref[...] = (mixed[...] / safe).astype(out_ref.dtype)
        log = jnp.where(some, high[...] * EXPONENT + jnp.log2(safe), NEVER)
        log_ref[pl.ds(head, 1), :] = jnp.transpose(jnp.broadcast_to(log, (rows, BLOCK)))[:1]

    everything = slice(0, rows)

    def reach(query_first):
        begin = jnp.int32(0)
        for genome in range(genomes):
            start = facts_ref[genome]
            begin = jnp.where(start <= query_first, jnp.maximum(begin, start), begin)
        return begin

    clear()

    @pl.when((shard == 1) & (reach(own_first) < rows))
    def _():
        update(everything, own_q[...], far_k[...], far_v[...], own_first, 0)

    for b in range(rows // BLOCK):
        here = slice(b * BLOCK, (b + 1) * BLOCK)
        upto = slice(0, (b + 1) * BLOCK)
        update(here, own_q[here], own_k[upto], own_v[upto], own_first + b * BLOCK, own_first)
    finish(own_o, own_l)

    for queries, query_shard, used, out_ref, log_ref in (
        (next_q, shard + 1, (shard == 1) | (shard == 2), next_o, next_l),
        (last_q, 3, shard == 1, last_o, last_l),
    ):
        query_first = query_shard * rows
        begin = reach(query_first)
        needed = used & (begin < own_first + rows)

        @pl.when(needed)
        def _():
            clear()
            update(everything, queries[...], own_k[...], own_v[...], query_first, own_first)

            @pl.when((shard == 1) & (begin < rows))
            def _():
                update(everything, queries[...], far_k[...], far_v[...], query_first, 0)

            finish(out_ref, log_ref)

        @pl.when(jnp.logical_not(needed))
        def _():
            out_ref[...] = jnp.zeros_like(out_ref)
            log_ref[pl.ds(head, 1), :] = jnp.full((1, rows), NEVER, jnp.float32)


def attend(facts, genomes, chunk, heads, own_q, next_q, last_q, own_k, own_v, far_k, far_v):
    rows = own_q.shape[0]
    whole = pl.BlockSpec((rows, HEAD_DIM), lambda h, facts_ref: (0, chunk * heads + h))
    piece = pl.BlockSpec((rows, HEAD_DIM), lambda h, facts_ref: (0, h))
    logs = pl.BlockSpec((heads, rows), lambda h, facts_ref: (0, 0))
    width = heads * HEAD_DIM
    return pl.pallas_call(
        partial(attend_kernel, genomes),
        out_shape=(
            jax.ShapeDtypeStruct((rows, width), jnp.float32),
            jax.ShapeDtypeStruct((rows, width), jnp.bfloat16),
            jax.ShapeDtypeStruct((rows, width), jnp.bfloat16),
            jax.ShapeDtypeStruct((heads, rows), jnp.float32),
            jax.ShapeDtypeStruct((heads, rows), jnp.float32),
            jax.ShapeDtypeStruct((heads, rows), jnp.float32),
        ),
        grid_spec=pltpu.PrefetchScalarGridSpec(
            num_scalar_prefetch=1,
            grid=(heads,),
            in_specs=[whole, piece, piece, whole, whole, piece, piece],
            out_specs=[piece, piece, piece, logs, logs, logs],
            scratch_shapes=[
                pltpu.VMEM((rows, 1), jnp.float32),
                pltpu.VMEM((rows, 1), jnp.float32),
                pltpu.VMEM((rows, HEAD_DIM), jnp.float32),
            ],
        ),
        compiler_params=pltpu.CompilerParams(vmem_limit_bytes=32 << 20),
        cost_estimate=pl.CostEstimate(
            flops=24 * rows * rows * width,
            bytes_accessed=rows * width * 22,
            transcendentals=6 * rows * rows * heads,
        ),
        name="attend",
    )(facts, own_q, next_q, last_q, own_k, own_v, far_k, far_v)


def combine_kernel(genomes, facts_ref, *refs):
    own_o, near_o, far_o, own_l, near_l, far_l = refs[-7:-1]
    out_ref = refs[-1]
    rows = own_o.shape[0]
    head = pl.program_id(0)
    shard = facts_ref[genomes]

    def column(log_ref):
        return jnp.transpose(jnp.broadcast_to(log_ref[pl.ds(head, 1), :], (BLOCK, rows)))

    own = column(own_l)
    near = jnp.where(shard >= 2, column(near_l), NEVER)
    far = jnp.where(shard == 3, column(far_l), NEVER)
    highest = jnp.maximum(own, jnp.maximum(near, far))
    own, near, far = jnp.exp2(own - highest), jnp.exp2(near - highest), jnp.exp2(far - highest)
    mixed = (
        own * own_o[...]
        + near * near_o[...].astype(jnp.float32)
        + far * far_o[...].astype(jnp.float32)
    )
    out_ref[...] = (mixed / (own + near + far)).astype(out_ref.dtype)


def combine(facts, genomes, chunk, heads, channels, earlier, *pieces):
    rows = pieces[0].shape[0]
    piece = pl.BlockSpec((rows, HEAD_DIM), lambda h, facts_ref: (0, h))
    logs = pl.BlockSpec((heads, rows), lambda h, facts_ref: (0, 0))
    held = () if earlier is None else (earlier,)
    return pl.pallas_call(
        partial(combine_kernel, genomes),
        out_shape=jax.ShapeDtypeStruct((rows, channels), jnp.bfloat16),
        grid_spec=pltpu.PrefetchScalarGridSpec(
            num_scalar_prefetch=1,
            grid=(heads,),
            in_specs=[pl.BlockSpec(memory_space=pl.ANY)] * len(held) + [piece] * 3 + [logs] * 3,
            out_specs=pl.BlockSpec(
                (rows, HEAD_DIM), lambda h, facts_ref: (0, chunk * heads + h)
            ),
        ),
        input_output_aliases={1: 0} if held else {},
        cost_estimate=pl.CostEstimate(
            flops=rows * heads * HEAD_DIM * 16,
            bytes_accessed=rows * heads * HEAD_DIM * 10,
            transcendentals=0,
        ),
        name="combine",
    )(facts, *held, *pieces)


def balanced_plan(
    hyena_query, hyena_key, hyena_value, filters, skip_gain, attn_query, attn_key, genome_starts
):
    rows, channels = hyena_key.shape
    genomes = genome_starts.shape[0]
    shard = lax.axis_index("ctx")
    facts = jnp.concatenate([genome_starts, jnp.full((1,), shard, jnp.int32)])
    tail = (
        hyena_key[rows - BLOCK :].astype(jnp.float32)
        * hyena_value[rows - BLOCK :].astype(jnp.float32)
    ).astype(jnp.bfloat16)
    halo = passed_along(tail, "ctx", 1)
    turned_taps = jnp.roll(filters[:, ::-1], 1, axis=1).astype(jnp.float32)
    mix = hyena(
        facts, genomes, hyena_query, hyena_key, hyena_value, halo, turned_taps, skip_gain[None, :]
    )
    heads = channels // HEAD_DIM // CHUNKS
    width = heads * HEAD_DIM
    attended = None
    parts = []
    for chunk in range(CHUNKS):
        here = slice(chunk * width, (chunk + 1) * width)
        queries = attn_query[:, here]
        far_k = lax.ppermute(attn_key[:, here], "ctx", [(0, 1)])
        next_q = lax.ppermute(queries, "ctx", [(2, 1), (3, 2)])
        last_q = lax.ppermute(queries, "ctx", [(3, 1)])
        far_v = lax.ppermute(mix[:, here], "ctx", [(0, 1)])
        own_o, next_o, last_o, own_l, next_l, last_l = attend(
            facts, genomes, chunk, heads, attn_query, next_q, last_q, attn_key, mix, far_k, far_v
        )
        parts.append(
            (
                own_o,
                lax.ppermute(next_o, "ctx", [(1, 2), (2, 3)]),
                lax.ppermute(last_o, "ctx", [(1, 3)]),
                own_l,
                lax.ppermute(next_l, "ctx", [(1, 2), (2, 3)]),
                lax.ppermute(last_l, "ctx", [(1, 3)]),
            )
        )
    for chunk in range(CHUNKS):
        attended = combine(facts, genomes, chunk, heads, channels, attended, *parts[chunk])
    return (mix, attended)


def solution(mesh):
    return jax.shard_map(
        balanced_plan if mesh.shape["ctx"] == 4 else gathered_plan,
        mesh=mesh,
        in_specs=(
            P(("rep", "ctx"), ("ch", "sub")),
            P(("rep", "ctx"), ("ch", "sub")),
            P(("rep", "ctx"), ("ch", "sub")),
            P(("ch", "sub"), None),
            P(("ch", "sub")),
            P(("rep", "ctx"), ("ch", "sub")),
            P(("rep", "ctx"), ("ch", "sub")),
            P("rep"),
        ),
        out_specs=(P(("rep", "ctx"), ("ch", "sub")), P(("rep", "ctx"), ("ch", "sub"))),
        check_vma=False,
    )
```

```python
from functools import partial
import math

import jax
import jax.numpy as jnp
from jax import lax
from jax.experimental import pallas as pl
from jax.experimental.pallas import tpu as pltpu
from jax.sharding import PartitionSpec as P

HEAD_DIM = 128


def passed_along(value, axis, by):
    devices = lax.axis_size(axis)
    pairs = [(i, i + by) for i in range(devices) if 0 <= i + by < devices]
    return lax.ppermute(value, axis, pairs)


def genome_index(positions, genome_starts):
    inside = genome_starts[None, :] <= positions[:, None]
    return jnp.sum(inside.astype(jnp.int32), axis=1) - 1


def genome_begin(positions, genome_starts):
    inside = genome_starts[None, :] <= positions[:, None]
    return jnp.max(jnp.where(inside, genome_starts[None, :], 0), axis=1)


def grouped_filter(product, parity, filters, left_pad):
    channels = product.shape[1]
    group_width = channels // filters.shape[0]
    kernel = jnp.repeat(filters, group_width, axis=0).T[::-1][:, None, :]
    nothing = jnp.zeros_like(product)
    even_rows = jnp.where((parity == 0)[:, None], product, nothing)
    odd_rows = jnp.where((parity == 1)[:, None], product, nothing)
    stacked = jnp.stack([even_rows, odd_rows])
    return lax.conv_general_dilated(
        stacked,
        kernel,
        (1,),
        [(left_pad, 0)],
        dimension_numbers=("NWC", "WIO", "NWC"),
        feature_group_count=channels,
        preferred_element_type=jnp.float32,
    )


def attend_update(carried, queries, query_pos, query_begin, key_heads, value_heads, key_pos):
    weighted, running_max, weight_sum = carried
    score_scale = 1.0 / math.sqrt(HEAD_DIM)
    scores = (
        jnp.einsum("qhd,khd->hqk", queries, key_heads, preferred_element_type=jnp.float32)
        * score_scale
    )
    visible = (key_pos[None, :] <= query_pos[:, None]) & (key_pos[None, :] >= query_begin[:, None])
    new_max = jnp.maximum(running_max, jnp.max(jnp.where(visible[None], scores, -1e30), axis=2))
    weights = jnp.exp(jnp.where(visible[None], scores - new_max[:, :, None], -1e30))
    mixed = jnp.einsum(
        "hqk,khd->hqd",
        weights.astype(jnp.bfloat16),
        value_heads,
        preferred_element_type=jnp.float32,
    )
    return (mixed, new_max, jnp.sum(weights, axis=2))


def keep_state(carried):
    return carried


def gathered_plan(
    hyena_query, hyena_key, hyena_value, filters, skip_gain, attn_query, attn_key, genome_starts
):
    local_rows, channels = hyena_key.shape
    taps = filters.shape[1]
    shard_first = lax.axis_index("ctx") * local_rows
    product = lax.optimization_barrier(
        (hyena_key.astype(jnp.float32) * hyena_value.astype(jnp.float32)).astype(jnp.bfloat16)
    )
    earlier = passed_along(product[local_rows - (taps - 1) :], "ctx", 1)
    extended = jnp.concatenate([earlier, product], axis=0)
    extended_pos = shard_first - (taps - 1) + jnp.arange(local_rows + taps - 1, dtype=jnp.int32)
    both_parities = grouped_filter(
        extended, genome_index(extended_pos, genome_starts) % 2, filters, 0
    )
    own_pos = shard_first + jnp.arange(local_rows, dtype=jnp.int32)
    own_parity = genome_index(own_pos, genome_starts) % 2
    filtered = jnp.where((own_parity == 0)[:, None], both_parities[0], both_parities[1])
    hyena_mix = (
        hyena_query.astype(jnp.float32)
        * (filtered + skip_gain[None, :] * product.astype(jnp.float32))
    ).astype(jnp.bfloat16)
    head_count = channels // HEAD_DIM
    queries = attn_query.reshape(local_rows, head_count, HEAD_DIM)
    pairs = [(queries, own_pos)]
    groups = [
        (group_queries, group_pos, genome_begin(group_pos, genome_starts))
        for group_queries, group_pos in pairs
    ]
    initial = tuple(
        (
            (
                jnp.zeros((head_count, group_pos.shape[0], HEAD_DIM), jnp.float32),
                jnp.full((head_count, group_pos.shape[0]), -1e30, jnp.float32),
                jnp.zeros((head_count, group_pos.shape[0]), jnp.float32),
            )
            for group_queries, group_pos, group_begin in groups
        )
    )
    offset_row = jnp.int32(0)
    keys_piece = lax.all_gather(attn_key, "ctx", axis=0, tiled=True)
    values_piece = lax.all_gather(hyena_mix, "ctx", axis=0, tiled=True)
    key_rows = keys_piece.shape[0]
    key_heads = keys_piece.reshape(key_rows, head_count, HEAD_DIM)
    value_heads = values_piece.reshape(key_rows, head_count, HEAD_DIM)
    key_pos = jnp.arange(key_rows, dtype=jnp.int32)
    updated = []
    for state_now, (group_queries, group_pos, group_begin) in zip(initial, groups):
        needed = (offset_row <= jnp.max(group_pos)) & (offset_row + key_rows > jnp.min(group_begin))
        update = partial(
            attend_update,
            queries=group_queries,
            query_pos=group_pos,
            query_begin=group_begin,
            key_heads=key_heads,
            value_heads=value_heads,
            key_pos=key_pos,
        )
        updated.append(lax.cond(needed, update, keep_state, state_now))
    results = tuple(updated)
    outputs = []
    for weighted, running_max, weight_sum in results:
        finished = (weighted / weight_sum[:, :, None]).astype(jnp.bfloat16)
        outputs.append(finished.transpose(1, 0, 2).reshape(weighted.shape[1], channels))
    attended = outputs[0]
    return (hyena_mix, attended)


NEVER = -1e29
BLOCK = 128
CHUNKS = 4
EXPONENT = math.log2(math.e) / math.sqrt(HEAD_DIM)


def begin_of(positions, facts_ref, genomes):
    begin = jnp.zeros_like(positions)
    for genome in range(genomes):
        start = facts_ref[genome]
        begin = jnp.where(start <= positions, jnp.maximum(begin, start), begin)
    return begin


def hyena_kernel(genomes, facts_ref, query_ref, key_ref, value_ref, halo_ref, taps_ref, gain_ref,
                 mix_ref, extended, masks):
    rows = key_ref.shape[0]
    blocks = rows // BLOCK
    groups = taps_ref.shape[0]
    group_width = BLOCK // groups

    @pl.when(pl.program_id(0) == 0)
    def _():
        first = facts_ref[genomes] * rows
        for b in range(blocks):
            i = lax.broadcasted_iota(jnp.int32, (BLOCK, 2 * BLOCK), 0)
            j = lax.broadcasted_iota(jnp.int32, (BLOCK, 2 * BLOCK), 1) - BLOCK
            begin = begin_of(i + (first + b * BLOCK), facts_ref, genomes)
            tap = i - j
            inside = (tap >= 0) & (tap < BLOCK) & (j + (first + b * BLOCK) >= begin)
            masks[b] = jnp.where(inside, 1.0, 0.0).astype(jnp.bfloat16)

    product = (key_ref[...].astype(jnp.float32) * value_ref[...].astype(jnp.float32)).astype(
        jnp.bfloat16
    )
    extended[:BLOCK] = halo_ref[...]
    extended[BLOCK:] = product
    lane_group = lax.broadcasted_iota(jnp.int32, (BLOCK, BLOCK), 1) // group_width
    totals = [jnp.zeros((BLOCK, BLOCK), jnp.float32) for b in range(blocks)]
    for g in range(groups):
        row = jnp.broadcast_to(taps_ref[g : g + 1, :], (BLOCK, BLOCK))
        turned = pltpu.roll(row, 0, 1, stride=1, stride_axis=0).astype(jnp.bfloat16)
        both = jnp.concatenate([turned, turned], axis=1)
        for b in range(blocks):
            band = both * masks[b]
            part = jnp.dot(
                band, extended[b * BLOCK : (b + 2) * BLOCK], preferred_element_type=jnp.float32
            )
            totals[b] = jnp.where(lane_group == g, part, totals[b])
    for b in range(blocks):
        here = slice(b * BLOCK, (b + 1) * BLOCK)
        wide = extended[(b + 1) * BLOCK : (b + 2) * BLOCK].astype(jnp.float32)
        mix_ref[here] = (
            query_ref[here].astype(jnp.float32) * (totals[b] + gain_ref[...] * wide)
        ).astype(jnp.bfloat16)


def hyena(facts, genomes, query, key, value, halo, turned_taps, skip_gain):
    rows, channels = key.shape
    groups = turned_taps.shape[0] * BLOCK // channels
    column = lambda c, facts_ref: (0, c)
    return pl.pallas_call(
        partial(hyena_kernel, genomes),
        out_shape=jax.ShapeDtypeStruct((rows, channels), jnp.bfloat16),
        grid_spec=pltpu.PrefetchScalarGridSpec(
            num_scalar_prefetch=1,
            grid=(channels // BLOCK,),
            in_specs=[
                pl.BlockSpec((rows, BLOCK), column),
                pl.BlockSpec((rows, BLOCK), column),
                pl.BlockSpec((rows, BLOCK), column),
                pl.BlockSpec((BLOCK, BLOCK), column),
                pl.BlockSpec((groups, BLOCK), lambda c, facts_ref: (c, 0)),
                pl.BlockSpec((1, BLOCK), column),
            ],
            out_specs=pl.BlockSpec((rows, BLOCK), column),
            scratch_shapes=[
                pltpu.VMEM((rows + BLOCK, BLOCK), jnp.bfloat16),
                pltpu.VMEM((rows // BLOCK, BLOCK, 2 * BLOCK), jnp.bfloat16),
            ],
        ),
        cost_estimate=pl.CostEstimate(
            flops=rows * channels * 2 * 2 * BLOCK * groups,
            bytes_accessed=rows * channels * 8,
            transcendentals=0,
        ),
        name="hyena",
    )(facts, query, key, value, halo, turned_taps, skip_gain)


def attend_block(queries, keys, values, bias):
    scores = bias + lax.dot_general(
        queries, keys, (((1,), (1,)), ((), ())), preferred_element_type=jnp.float32
    )
    highest = jnp.maximum(jnp.max(scores, axis=1, keepdims=True), NEVER)
    weights = jnp.exp2((scores - highest) * EXPONENT).astype(jnp.bfloat16)
    mixed = jnp.dot(weights, values, preferred_element_type=jnp.float32)
    summed = mixed[:, HEAD_DIM:]
    some = summed > 0
    safe = jnp.where(some, summed, 1.0)
    log = jnp.where(some, highest * EXPONENT + jnp.log2(safe), NEVER)
    return mixed[:, :HEAD_DIM] / safe, log


def attend_kernel(genomes, facts_ref, own_q, next_q, last_q, own_k, own_v, far_k, far_v,
                  own_o, next_o, last_o, own_l, next_l, last_l, queries, keys, values, bias,
                  mixed, logs):
    rows = own_q.shape[0]
    per_shard = rows // BLOCK
    head = pl.program_id(0)
    shard = facts_ref[genomes]
    own_first = shard * rows
    base = own_first - rows
    limit = jnp.where(shard == 1, base, own_first)
    steps = per_shard * jnp.where(shard == 1, 3, jnp.where(shard == 2, 2, 1))

    def rows_of(step):
        return pl.ds(pl.multiple_of(step * BLOCK, BLOCK), BLOCK)

    @pl.when(head == 0)
    def _():
        values[:, HEAD_DIM:] = jnp.ones((2 * rows, HEAD_DIM), jnp.bfloat16)
        logs[...] = jnp.full_like(logs, NEVER)

        def fill(step, nothing):
            query_pos = own_first + step * BLOCK + lax.broadcasted_iota(jnp.int32, (BLOCK, 1), 0)
            begin = jnp.maximum(begin_of(query_pos, facts_ref, genomes), limit)
            key_pos = base + lax.broadcasted_iota(jnp.int32, (BLOCK, 2 * rows), 1)
            visible = (key_pos >= begin) & (key_pos <= query_pos)
            bias[rows_of(step), :] = jnp.where(visible, 0.0, 10 * NEVER)
            return nothing

        lax.fori_loop(0, steps, fill, 0)

    for slot, ref in enumerate((own_q, next_q, last_q)):
        queries[slot * rows : (slot + 1) * rows] = ref[...]
    for slot, (k_ref, v_ref) in enumerate(((far_k, far_v), (own_k, own_v))):
        here = slice(slot * rows, (slot + 1) * rows)
        keys[here] = k_ref[...]
        values[here, :HEAD_DIM] = v_ref[...]

    def one_step(step, nothing):
        query_first = own_first + step * BLOCK
        begin = limit
        for genome in range(genomes):
            start = facts_ref[genome]
            begin = jnp.where(start <= query_first, jnp.maximum(begin, start), begin)
        first = (begin - base) // BLOCK
        last = jnp.minimum(query_first + BLOCK, own_first + rows)
        count = (last - base) // BLOCK - first

        @pl.when(count <= 0)
        def _():
            mixed[rows_of(step), :] = jnp.zeros((BLOCK, HEAD_DIM), jnp.float32)

        for blocks in range(1, 2 * per_shard + 1):

            @pl.when(count == blocks)
            def _():
                span = pl.ds(pl.multiple_of(first * BLOCK, BLOCK), blocks * BLOCK)
                out, log = attend_block(
                    queries[rows_of(step), :], keys[span, :], values[span, :], bias[rows_of(step), span]
                )
                mixed[rows_of(step), :] = out
                lane = lax.broadcasted_iota(jnp.int32, (BLOCK, BLOCK), 1)
                logs[rows_of(step), :] = jnp.where(lane == head, log, logs[rows_of(step), :])

        return nothing

    lax.fori_loop(0, steps, one_step, 0)
    for slot, ref in enumerate((own_o, next_o, last_o)):
        ref[...] = mixed[slot * rows : (slot + 1) * rows].astype(ref.dtype)

    @pl.when(head == pl.num_programs(0) - 1)
    def _():
        for slot, ref in enumerate((own_l, next_l, last_l)):
            ref[...] = jnp.transpose(logs[slot * rows : (slot + 1) * rows])[:8]


def attend(facts, genomes, chunk, heads, own_q, next_q, last_q, own_k, own_v, far_k, far_v):
    rows = own_q.shape[0]
    whole = pl.BlockSpec((rows, HEAD_DIM), lambda h, facts_ref: (0, chunk * heads + h))
    piece = pl.BlockSpec((rows, HEAD_DIM), lambda h, facts_ref: (0, h))
    logs = pl.BlockSpec((8, rows), lambda h, facts_ref: (0, 0))
    width = heads * HEAD_DIM
    return pl.pallas_call(
        partial(attend_kernel, genomes),
        out_shape=(
            jax.ShapeDtypeStruct((rows, width), jnp.float32),
            jax.ShapeDtypeStruct((rows, width), jnp.bfloat16),
            jax.ShapeDtypeStruct((rows, width), jnp.bfloat16),
            jax.ShapeDtypeStruct((8, rows), jnp.float32),
            jax.ShapeDtypeStruct((8, rows), jnp.float32),
            jax.ShapeDtypeStruct((8, rows), jnp.float32),
        ),
        grid_spec=pltpu.PrefetchScalarGridSpec(
            num_scalar_prefetch=1,
            grid=(heads,),
            in_specs=[whole, piece, piece, whole, whole, piece, piece],
            out_specs=[piece, piece, piece, logs, logs, logs],
            scratch_shapes=[
                pltpu.VMEM((3 * rows, HEAD_DIM), jnp.bfloat16),
                pltpu.VMEM((2 * rows, HEAD_DIM), jnp.bfloat16),
                pltpu.VMEM((2 * rows, 2 * HEAD_DIM), jnp.bfloat16),
                pltpu.VMEM((3 * rows, 2 * rows), jnp.float32),
                pltpu.VMEM((3 * rows, HEAD_DIM), jnp.float32),
                pltpu.VMEM((3 * rows, BLOCK), jnp.float32),
            ],
        ),
        compiler_params=pltpu.CompilerParams(vmem_limit_bytes=32 << 20),
        cost_estimate=pl.CostEstimate(
            flops=12 * rows * rows * width,
            bytes_accessed=rows * width * 22,
            transcendentals=3 * rows * rows * heads,
        ),
        name="attend",
    )(facts, own_q, next_q, last_q, own_k, own_v, far_k, far_v)


def combine_kernel(genomes, facts_ref, *refs):
    own_o, near_o, far_o, own_l, near_l, far_l = refs[-7:-1]
    out_ref = refs[-1]
    width = own_o.shape[1]
    shard = facts_ref[genomes]
    own = own_l[...]
    near = jnp.where(shard >= 2, near_l[...], NEVER)
    far = jnp.where(shard == 3, far_l[...], NEVER)
    highest = jnp.maximum(own, jnp.maximum(near, far))
    shares = [jnp.exp2(log - highest) for log in (own, near, far)]
    whole = shares[0] + shares[1] + shares[2]
    columns = [
        jnp.transpose(jnp.concatenate([share / whole] + [jnp.zeros((BLOCK - 8, BLOCK), jnp.float32)]))
        for share in shares
    ]
    for head in range(width // HEAD_DIM):
        here = slice(head * HEAD_DIM, (head + 1) * HEAD_DIM)
        mixed = columns[0][:, head : head + 1] * own_o[:, here]
        for column, ref in ((columns[1], near_o), (columns[2], far_o)):
            mixed += column[:, head : head + 1] * ref[:, here].astype(jnp.float32)
        out_ref[:, here] = mixed.astype(out_ref.dtype)


def combine(facts, genomes, chunk, heads, channels, earlier, *pieces):
    rows = pieces[0].shape[0]
    width = heads * HEAD_DIM
    piece = pl.BlockSpec((BLOCK, width), lambda r, facts_ref: (r, 0))
    logs = pl.BlockSpec((8, BLOCK), lambda r, facts_ref: (0, r))
    held = () if earlier is None else (earlier,)
    return pl.pallas_call(
        partial(combine_kernel, genomes),
        out_shape=jax.ShapeDtypeStruct((rows, channels), jnp.bfloat16),
        grid_spec=pltpu.PrefetchScalarGridSpec(
            num_scalar_prefetch=1,
            grid=(rows // BLOCK,),
            in_specs=[pl.BlockSpec(memory_space=pl.ANY)] * len(held) + [piece] * 3 + [logs] * 3,
            out_specs=pl.BlockSpec((BLOCK, width), lambda r, facts_ref: (r, chunk)),
        ),
        input_output_aliases={1: 0} if held else {},
        cost_estimate=pl.CostEstimate(
            flops=rows * heads * HEAD_DIM * 16,
            bytes_accessed=rows * heads * HEAD_DIM * 10,
            transcendentals=0,
        ),
        name="combine",
    )(facts, *held, *pieces)


def balanced_plan(
    hyena_query, hyena_key, hyena_value, filters, skip_gain, attn_query, attn_key, genome_starts
):
    rows, channels = hyena_key.shape
    genomes = genome_starts.shape[0]
    shard = lax.axis_index("ctx")
    facts = jnp.concatenate([genome_starts, jnp.full((1,), shard, jnp.int32)])
    tail = (
        hyena_key[rows - BLOCK :].astype(jnp.float32)
        * hyena_value[rows - BLOCK :].astype(jnp.float32)
    ).astype(jnp.bfloat16)
    halo = passed_along(tail, "ctx", 1)
    turned_taps = jnp.roll(filters[:, ::-1], 1, axis=1).astype(jnp.float32)
    mix = hyena(
        facts, genomes, hyena_query, hyena_key, hyena_value, halo, turned_taps, skip_gain[None, :]
    )
    heads = channels // HEAD_DIM // CHUNKS
    width = heads * HEAD_DIM
    attended = None
    parts = []
    for chunk in range(CHUNKS):
        here = slice(chunk * width, (chunk + 1) * width)
        queries = attn_query[:, here]
        far_k = lax.ppermute(attn_key[:, here], "ctx", [(0, 1)])
        next_q = lax.ppermute(queries, "ctx", [(2, 1), (3, 2)])
        last_q = lax.ppermute(queries, "ctx", [(3, 1)])
        far_v = lax.ppermute(mix[:, here], "ctx", [(0, 1)])
        own_o, next_o, last_o, own_l, next_l, last_l = attend(
            facts, genomes, chunk, heads, attn_query, next_q, last_q, attn_key, mix, far_k, far_v
        )
        parts.append(
            (
                own_o,
                lax.ppermute(next_o, "ctx", [(1, 2), (2, 3)]),
                lax.ppermute(last_o, "ctx", [(1, 3)]),
                own_l,
                lax.ppermute(next_l, "ctx", [(1, 2), (2, 3)]),
                lax.ppermute(last_l, "ctx", [(1, 3)]),
            )
        )
    for chunk in range(CHUNKS):
        attended = combine(facts, genomes, chunk, heads, channels, attended, *parts[chunk])
    return (mix, attended)


def solution(mesh):
    return jax.shard_map(
        balanced_plan if mesh.shape["ctx"] == 4 else gathered_plan,
        mesh=mesh,
        in_specs=(
            P(("rep", "ctx"), ("ch", "sub")),
            P(("rep", "ctx"), ("ch", "sub")),
            P(("rep", "ctx"), ("ch", "sub")),
            P(("ch", "sub"), None),
            P(("ch", "sub")),
            P(("rep", "ctx"), ("ch", "sub")),
            P(("rep", "ctx"), ("ch", "sub")),
            P("rep"),
        ),
        out_specs=(P(("rep", "ctx"), ("ch", "sub")), P(("rep", "ctx"), ("ch", "sub"))),
        check_vma=False,
    )
```

```python
from functools import partial
import math

import jax
import jax.numpy as jnp
from jax import lax
from jax.experimental import pallas as pl
from jax.experimental.pallas import tpu as pltpu
from jax.sharding import PartitionSpec as P

HEAD_DIM = 128


def passed_along(value, axis, by):
    devices = lax.axis_size(axis)
    pairs = [(i, i + by) for i in range(devices) if 0 <= i + by < devices]
    return lax.ppermute(value, axis, pairs)


def genome_index(positions, genome_starts):
    inside = genome_starts[None, :] <= positions[:, None]
    return jnp.sum(inside.astype(jnp.int32), axis=1) - 1


def genome_begin(positions, genome_starts):
    inside = genome_starts[None, :] <= positions[:, None]
    return jnp.max(jnp.where(inside, genome_starts[None, :], 0), axis=1)


def grouped_filter(product, parity, filters, left_pad):
    channels = product.shape[1]
    group_width = channels // filters.shape[0]
    kernel = jnp.repeat(filters, group_width, axis=0).T[::-1][:, None, :]
    nothing = jnp.zeros_like(product)
    even_rows = jnp.where((parity == 0)[:, None], product, nothing)
    odd_rows = jnp.where((parity == 1)[:, None], product, nothing)
    stacked = jnp.stack([even_rows, odd_rows])
    return lax.conv_general_dilated(
        stacked,
        kernel,
        (1,),
        [(left_pad, 0)],
        dimension_numbers=("NWC", "WIO", "NWC"),
        feature_group_count=channels,
        preferred_element_type=jnp.float32,
    )


def attend_update(carried, queries, query_pos, query_begin, key_heads, value_heads, key_pos):
    weighted, running_max, weight_sum = carried
    score_scale = 1.0 / math.sqrt(HEAD_DIM)
    scores = (
        jnp.einsum("qhd,khd->hqk", queries, key_heads, preferred_element_type=jnp.float32)
        * score_scale
    )
    visible = (key_pos[None, :] <= query_pos[:, None]) & (key_pos[None, :] >= query_begin[:, None])
    new_max = jnp.maximum(running_max, jnp.max(jnp.where(visible[None], scores, -1e30), axis=2))
    weights = jnp.exp(jnp.where(visible[None], scores - new_max[:, :, None], -1e30))
    mixed = jnp.einsum(
        "hqk,khd->hqd",
        weights.astype(jnp.bfloat16),
        value_heads,
        preferred_element_type=jnp.float32,
    )
    return (mixed, new_max, jnp.sum(weights, axis=2))


def keep_state(carried):
    return carried


def gathered_plan(
    hyena_query, hyena_key, hyena_value, filters, skip_gain, attn_query, attn_key, genome_starts
):
    local_rows, channels = hyena_key.shape
    taps = filters.shape[1]
    shard_first = lax.axis_index("ctx") * local_rows
    product = lax.optimization_barrier(
        (hyena_key.astype(jnp.float32) * hyena_value.astype(jnp.float32)).astype(jnp.bfloat16)
    )
    earlier = passed_along(product[local_rows - (taps - 1) :], "ctx", 1)
    extended = jnp.concatenate([earlier, product], axis=0)
    extended_pos = shard_first - (taps - 1) + jnp.arange(local_rows + taps - 1, dtype=jnp.int32)
    both_parities = grouped_filter(
        extended, genome_index(extended_pos, genome_starts) % 2, filters, 0
    )
    own_pos = shard_first + jnp.arange(local_rows, dtype=jnp.int32)
    own_parity = genome_index(own_pos, genome_starts) % 2
    filtered = jnp.where((own_parity == 0)[:, None], both_parities[0], both_parities[1])
    hyena_mix = (
        hyena_query.astype(jnp.float32)
        * (filtered + skip_gain[None, :] * product.astype(jnp.float32))
    ).astype(jnp.bfloat16)
    head_count = channels // HEAD_DIM
    queries = attn_query.reshape(local_rows, head_count, HEAD_DIM)
    pairs = [(queries, own_pos)]
    groups = [
        (group_queries, group_pos, genome_begin(group_pos, genome_starts))
        for group_queries, group_pos in pairs
    ]
    initial = tuple(
        (
            (
                jnp.zeros((head_count, group_pos.shape[0], HEAD_DIM), jnp.float32),
                jnp.full((head_count, group_pos.shape[0]), -1e30, jnp.float32),
                jnp.zeros((head_count, group_pos.shape[0]), jnp.float32),
            )
            for group_queries, group_pos, group_begin in groups
        )
    )
    offset_row = jnp.int32(0)
    keys_piece = lax.all_gather(attn_key, "ctx", axis=0, tiled=True)
    values_piece = lax.all_gather(hyena_mix, "ctx", axis=0, tiled=True)
    key_rows = keys_piece.shape[0]
    key_heads = keys_piece.reshape(key_rows, head_count, HEAD_DIM)
    value_heads = values_piece.reshape(key_rows, head_count, HEAD_DIM)
    key_pos = jnp.arange(key_rows, dtype=jnp.int32)
    updated = []
    for state_now, (group_queries, group_pos, group_begin) in zip(initial, groups):
        needed = (offset_row <= jnp.max(group_pos)) & (offset_row + key_rows > jnp.min(group_begin))
        update = partial(
            attend_update,
            queries=group_queries,
            query_pos=group_pos,
            query_begin=group_begin,
            key_heads=key_heads,
            value_heads=value_heads,
            key_pos=key_pos,
        )
        updated.append(lax.cond(needed, update, keep_state, state_now))
    results = tuple(updated)
    outputs = []
    for weighted, running_max, weight_sum in results:
        finished = (weighted / weight_sum[:, :, None]).astype(jnp.bfloat16)
        outputs.append(finished.transpose(1, 0, 2).reshape(weighted.shape[1], channels))
    attended = outputs[0]
    return (hyena_mix, attended)


NEVER = -1e29
BLOCK = 128
CHUNKS = 4
AHEAD = 2
EXPONENT = math.log2(math.e) / math.sqrt(HEAD_DIM)


def begin_of(positions, facts_ref, genomes):
    begin = jnp.zeros_like(positions)
    for genome in range(genomes):
        start = facts_ref[genome]
        begin = jnp.where(start <= positions, jnp.maximum(begin, start), begin)
    return begin


def hyena_kernel(genomes, facts_ref, query_ref, key_ref, value_ref, halo_ref, taps_ref, gain_ref,
                 mix_ref, extended, masks, bands):
    rows = key_ref.shape[0]
    blocks = rows // BLOCK
    groups = taps_ref.shape[0]
    group_width = BLOCK // groups

    @pl.when(pl.program_id(0) == 0)
    def _():
        first = facts_ref[genomes] * rows
        for b in range(blocks):
            i = lax.broadcasted_iota(jnp.int32, (BLOCK, 2 * BLOCK), 0)
            j = lax.broadcasted_iota(jnp.int32, (BLOCK, 2 * BLOCK), 1) - BLOCK
            begin = begin_of(i + (first + b * BLOCK), facts_ref, genomes)
            tap = i - j
            inside = (tap >= 0) & (tap < BLOCK) & (j + (first + b * BLOCK) >= begin)
            masks[b] = jnp.where(inside, 1.0, 0.0).astype(jnp.bfloat16)

    product = (key_ref[...].astype(jnp.float32) * value_ref[...].astype(jnp.float32)).astype(
        jnp.bfloat16
    )
    extended[:BLOCK] = halo_ref[...]
    extended[BLOCK:] = product
    lane_group = lax.broadcasted_iota(jnp.int32, (BLOCK, BLOCK), 1) // group_width
    for g in range(groups):
        row = jnp.broadcast_to(taps_ref[g : g + 1, :], (BLOCK, BLOCK))
        turned = pltpu.roll(row, 0, 1, stride=1, stride_axis=0).astype(jnp.bfloat16)
        both = jnp.concatenate([turned, turned], axis=1)
        for b in range(blocks):
            bands[b, g * BLOCK : (g + 1) * BLOCK] = both * masks[b]
    totals = []
    for b in range(blocks):
        parts = jnp.dot(
            bands[b], extended[b * BLOCK : (b + 2) * BLOCK], preferred_element_type=jnp.float32
        )
        picked = parts[:BLOCK]
        for g in range(1, groups):
            picked = jnp.where(lane_group == g, parts[g * BLOCK : (g + 1) * BLOCK], picked)
        totals.append(picked)
    for b in range(blocks):
        here = slice(b * BLOCK, (b + 1) * BLOCK)
        wide = extended[(b + 1) * BLOCK : (b + 2) * BLOCK].astype(jnp.float32)
        mix_ref[here] = (
            query_ref[here].astype(jnp.float32) * (totals[b] + gain_ref[...] * wide)
        ).astype(jnp.bfloat16)


def hyena(facts, genomes, query, key, value, halo, turned_taps, skip_gain):
    rows, channels = key.shape
    groups = turned_taps.shape[0] * BLOCK // channels
    column = lambda c, facts_ref: (0, c)
    return pl.pallas_call(
        partial(hyena_kernel, genomes),
        out_shape=jax.ShapeDtypeStruct((rows, channels), jnp.bfloat16),
        grid_spec=pltpu.PrefetchScalarGridSpec(
            num_scalar_prefetch=1,
            grid=(channels // BLOCK,),
            in_specs=[
                pl.BlockSpec((rows, BLOCK), column),
                pl.BlockSpec((rows, BLOCK), column),
                pl.BlockSpec((rows, BLOCK), column),
                pl.BlockSpec((BLOCK, BLOCK), column),
                pl.BlockSpec((groups, BLOCK), lambda c, facts_ref: (c, 0)),
                pl.BlockSpec((1, BLOCK), column),
            ],
            out_specs=pl.BlockSpec((rows, BLOCK), column),
            scratch_shapes=[
                pltpu.VMEM((rows + BLOCK, BLOCK), jnp.bfloat16),
                pltpu.VMEM((rows // BLOCK, BLOCK, 2 * BLOCK), jnp.bfloat16),
                pltpu.VMEM((rows // BLOCK, groups * BLOCK, 2 * BLOCK), jnp.bfloat16),
            ],
        ),
        cost_estimate=pl.CostEstimate(
            flops=rows * channels * 2 * 2 * BLOCK * groups,
            bytes_accessed=rows * channels * 8,
            transcendentals=0,
        ),
        name="hyena",
    )(facts, query, key, value, halo, turned_taps, skip_gain)


def attend_block(queries, keys, values, bias):
    scores = bias + lax.dot_general(
        queries, keys, (((1,), (1,)), ((), ())), preferred_element_type=jnp.float32
    )
    highest = jnp.maximum(jnp.max(scores, axis=1, keepdims=True), NEVER)
    weights = jnp.exp2((scores - highest) * EXPONENT).astype(jnp.bfloat16)
    mixed = jnp.dot(weights, values, preferred_element_type=jnp.float32)
    summed = mixed[:, HEAD_DIM:]
    some = summed > 0
    safe = jnp.where(some, summed, 1.0)
    log = jnp.where(some, highest * EXPONENT + jnp.log2(safe), NEVER)
    return mixed[:, :HEAD_DIM] / safe, log


def pieces_of(log):
    high = log.astype(jnp.bfloat16)
    rest = log - high.astype(jnp.float32)
    middle = rest.astype(jnp.bfloat16)
    low = (rest - middle.astype(jnp.float32)).astype(jnp.bfloat16)
    return jnp.concatenate([high, middle, low, jnp.zeros_like(low)])


def joined(pieces):
    wide = pieces.astype(jnp.float32)
    return wide[:8] + wide[8:16] + wide[16:24]


def attend_kernel(genomes, facts_ref, own_q, next_q, last_q, own_k, own_v, far_k, far_v,
                  own_o, next_o, last_o, own_l, queries, keys, values, bias, mixed, logs):
    rows, width = own_q.shape
    heads = width // HEAD_DIM
    per_shard = rows // BLOCK
    shard = facts_ref[genomes]
    own_first = shard * rows
    base = own_first - rows
    limit = jnp.where(shard == 1, base, own_first)
    steps = per_shard * jnp.where(shard == 1, 3, jnp.where(shard == 2, 2, 1))

    def rows_of(step):
        return pl.ds(pl.multiple_of(step * BLOCK, BLOCK), BLOCK)

    logs[...] = jnp.full_like(logs, NEVER)

    def fill(step, nothing):
        query_pos = own_first + step * BLOCK + lax.broadcasted_iota(jnp.int32, (BLOCK, 1), 0)
        begin = jnp.maximum(begin_of(query_pos, facts_ref, genomes), limit)
        key_pos = base + lax.broadcasted_iota(jnp.int32, (BLOCK, 2 * rows), 1)
        visible = (key_pos >= begin) & (key_pos <= query_pos)
        bias[rows_of(step), :] = jnp.where(visible, 0.0, 10 * NEVER)
        return nothing

    lax.fori_loop(0, steps, fill, 0)
    for slot, ref in enumerate((own_q, next_q, last_q)):
        queries[slot * rows : (slot + 1) * rows] = ref[...]
    for slot, (k_ref, v_ref) in enumerate(((far_k, far_v), (own_k, own_v))):
        here = slice(slot * rows, (slot + 1) * rows)
        keys[here] = k_ref[...]
        for head in range(heads):
            first = 2 * head * HEAD_DIM
            values[here, first : first + HEAD_DIM] = v_ref[:, head * HEAD_DIM : (head + 1) * HEAD_DIM]
            values[here, first + HEAD_DIM : first + 2 * HEAD_DIM] = jnp.ones(
                (rows, HEAD_DIM), jnp.bfloat16
            )

    def one_step(step, nothing):
        query_first = own_first + step * BLOCK
        begin = limit
        for genome in range(genomes):
            start = facts_ref[genome]
            begin = jnp.where(start <= query_first, jnp.maximum(begin, start), begin)
        first = (begin - base) // BLOCK
        last = jnp.minimum(query_first + BLOCK, own_first + rows)
        count = (last - base) // BLOCK - first

        @pl.when(count <= 0)
        def _():
            mixed[rows_of(step), :] = jnp.zeros((BLOCK, width), jnp.float32)

        for blocks in range(1, 2 * per_shard + 1):

            @pl.when(count == blocks)
            def _():
                span = pl.ds(pl.multiple_of(first * BLOCK, BLOCK), blocks * BLOCK)
                mask = bias[rows_of(step), span]
                lane = lax.broadcasted_iota(jnp.int32, (BLOCK, BLOCK), 1)
                gathered = jnp.full((BLOCK, BLOCK), NEVER, jnp.float32)
                for head in range(heads):
                    here = slice(head * HEAD_DIM, (head + 1) * HEAD_DIM)
                    both = slice(2 * head * HEAD_DIM, 2 * (head + 1) * HEAD_DIM)
                    out, log = attend_block(
                        queries[rows_of(step), here], keys[span, here], values[span, both], mask
                    )
                    mixed[rows_of(step), here] = out
                    gathered = jnp.where(lane == head, log, gathered)
                logs[rows_of(step), :] = gathered

        return nothing

    lax.fori_loop(0, steps, one_step, 0)
    own_o[...] = mixed[:rows]
    own_l[...] = jnp.transpose(logs[:rows])[:8]
    for slot, ref, used in ((1, next_o, (shard == 1) | (shard == 2)), (2, last_o, shard == 1)):

        @pl.when(used)
        def _():
            here = slice(slot * rows, (slot + 1) * rows)
            ref[:rows] = mixed[here].astype(ref.dtype)
            ref[rows:, :rows] = pieces_of(jnp.transpose(logs[here])[:8])
            ref[rows:, rows:] = jnp.zeros((32, width - rows), ref.dtype)

        @pl.when(jnp.logical_not(used))
        def _():
            ref[...] = jnp.zeros_like(ref)


def attend(facts, genomes, chunk, heads, own_q, next_q, last_q, own_k, own_v, far_k, far_v):
    rows = own_q.shape[0]
    width = heads * HEAD_DIM
    whole = pl.BlockSpec((rows, width), lambda h, facts_ref: (0, chunk))
    piece = pl.BlockSpec((rows, width), lambda h, facts_ref: (0, 0))
    sent = pl.BlockSpec((rows + 32, width), lambda h, facts_ref: (0, 0))
    logs = pl.BlockSpec((8, rows), lambda h, facts_ref: (0, 0))
    return pl.pallas_call(
        partial(attend_kernel, genomes),
        out_shape=(
            jax.ShapeDtypeStruct((rows, width), jnp.float32),
            jax.ShapeDtypeStruct((rows + 32, width), jnp.bfloat16),
            jax.ShapeDtypeStruct((rows + 32, width), jnp.bfloat16),
            jax.ShapeDtypeStruct((8, rows), jnp.float32),
        ),
        grid_spec=pltpu.PrefetchScalarGridSpec(
            num_scalar_prefetch=1,
            grid=(1,),
            in_specs=[whole, piece, piece, whole, whole, piece, piece],
            out_specs=[piece, sent, sent, logs],
            scratch_shapes=[
                pltpu.VMEM((3 * rows, width), jnp.bfloat16),
                pltpu.VMEM((2 * rows, width), jnp.bfloat16),
                pltpu.VMEM((2 * rows, 2 * width), jnp.bfloat16),
                pltpu.VMEM((3 * rows, 2 * rows), jnp.float32),
                pltpu.VMEM((3 * rows, width), jnp.float32),
                pltpu.VMEM((3 * rows, BLOCK), jnp.float32),
            ],
        ),
        compiler_params=pltpu.CompilerParams(vmem_limit_bytes=32 << 20),
        cost_estimate=pl.CostEstimate(
            flops=12 * rows * rows * width,
            bytes_accessed=rows * width * 22,
            transcendentals=3 * rows * rows * heads,
        ),
        name="attend",
    )(facts, own_q, next_q, last_q, own_k, own_v, far_k, far_v)


def combine_kernel(genomes, heads, facts_ref, *refs):
    out_ref = refs[-1]
    width = heads * HEAD_DIM
    shard = facts_ref[genomes]
    for chunk in range(CHUNKS):
        own_o, near_o, far_o, own_l, near_l, far_l = refs[6 * chunk : 6 * chunk + 6]
        own = own_l[...]
        near = jnp.where(shard >= 2, joined(near_l[...]), NEVER)
        far = jnp.where(shard == 3, joined(far_l[...]), NEVER)
        highest = jnp.maximum(own, jnp.maximum(near, far))
        shares = [jnp.exp2(log - highest) for log in (own, near, far)]
        whole = shares[0] + shares[1] + shares[2]
        columns = [
            jnp.transpose(
                jnp.concatenate([share / whole, jnp.zeros((BLOCK - 8, BLOCK), jnp.float32)])
            )
            for share in shares
        ]
        for head in range(heads):
            here = slice(head * HEAD_DIM, (head + 1) * HEAD_DIM)
            mixed = columns[0][:, head : head + 1] * own_o[:, here]
            for column, ref in ((columns[1], near_o), (columns[2], far_o)):
                mixed += column[:, head : head + 1] * ref[:, here].astype(jnp.float32)
            first = chunk * width + head * HEAD_DIM
            out_ref[:, first : first + HEAD_DIM] = mixed.astype(out_ref.dtype)


def combine(facts, genomes, heads, channels, parts):
    rows, width = parts[0][0].shape
    piece = pl.BlockSpec((BLOCK, width), lambda r, facts_ref: (r, 0))
    own = pl.BlockSpec((8, BLOCK), lambda r, facts_ref: (0, r))
    logs = pl.BlockSpec((32, BLOCK), lambda r, facts_ref: (rows // 32, r))
    operands = [x for o, near, far, l in parts for x in (o, near, far, l, near, far)]
    return pl.pallas_call(
        partial(combine_kernel, genomes, heads),
        out_shape=jax.ShapeDtypeStruct((rows, channels), jnp.bfloat16),
        grid_spec=pltpu.PrefetchScalarGridSpec(
            num_scalar_prefetch=1,
            grid=(rows // BLOCK,),
            in_specs=[piece, piece, piece, own, logs, logs] * CHUNKS,
            out_specs=pl.BlockSpec((BLOCK, channels), lambda r, facts_ref: (r, 0)),
        ),
        cost_estimate=pl.CostEstimate(
            flops=rows * channels * 16, bytes_accessed=rows * channels * 10, transcendentals=0
        ),
        name="combine",
    )(facts, *operands)


def balanced_plan(
    hyena_query, hyena_key, hyena_value, filters, skip_gain, attn_query, attn_key, genome_starts
):
    rows, channels = hyena_key.shape
    genomes = genome_starts.shape[0]
    shard = lax.axis_index("ctx")
    facts = jnp.concatenate([genome_starts, jnp.full((1,), shard, jnp.int32)])
    tail = (
        hyena_key[rows - BLOCK :].astype(jnp.float32)
        * hyena_value[rows - BLOCK :].astype(jnp.float32)
    ).astype(jnp.bfloat16)
    halo = passed_along(tail, "ctx", 1)
    turned_taps = jnp.roll(filters[:, ::-1], 1, axis=1).astype(jnp.float32)
    mix = hyena(
        facts, genomes, hyena_query, hyena_key, hyena_value, halo, turned_taps, skip_gain[None, :]
    )
    heads = channels // HEAD_DIM // CHUNKS
    width = heads * HEAD_DIM
    parts = []
    for chunk in range(CHUNKS):
        here = slice(chunk * width, (chunk + 1) * width)
        pieces = (attn_key[:, here], attn_query[:, here], mix[:, here])
        if chunk >= AHEAD:
            pieces, parts[chunk - AHEAD] = lax.optimization_barrier((pieces, parts[chunk - AHEAD]))
        far_k = lax.ppermute(pieces[0], "ctx", [(0, 1)])
        next_q = lax.ppermute(pieces[1], "ctx", [(2, 1), (3, 2)])
        last_q = lax.ppermute(pieces[1], "ctx", [(3, 1)])
        far_v = lax.ppermute(pieces[2], "ctx", [(0, 1)])
        parts.append(
            attend(
                facts, genomes, chunk, heads, attn_query, next_q, last_q, attn_key, mix, far_k, far_v
            )
        )
    returned = [
        (
            own_o,
            lax.ppermute(next_o, "ctx", [(1, 2), (2, 3)]),
            lax.ppermute(last_o, "ctx", [(1, 3)]),
            own_l,
        )
        for own_o, next_o, last_o, own_l in parts
    ]
    return (mix, combine(facts, genomes, heads, channels, returned))


def solution(mesh):
    return jax.shard_map(
        balanced_plan if mesh.shape["ctx"] == 4 else gathered_plan,
        mesh=mesh,
        in_specs=(
            P(("rep", "ctx"), ("ch", "sub")),
            P(("rep", "ctx"), ("ch", "sub")),
            P(("rep", "ctx"), ("ch", "sub")),
            P(("ch", "sub"), None),
            P(("ch", "sub")),
            P(("rep", "ctx"), ("ch", "sub")),
            P(("rep", "ctx"), ("ch", "sub")),
            P("rep"),
        ),
        out_specs=(P(("rep", "ctx"), ("ch", "sub")), P(("rep", "ctx"), ("ch", "sub"))),
        check_vma=False,
    )
```

```python
from functools import partial
import math

import jax
import jax.numpy as jnp
from jax import lax
from jax.experimental import pallas as pl
from jax.experimental.pallas import tpu as pltpu
from jax.sharding import PartitionSpec as P

HEAD_DIM = 128


def passed_along(value, axis, by):
    devices = lax.axis_size(axis)
    pairs = [(i, i + by) for i in range(devices) if 0 <= i + by < devices]
    return lax.ppermute(value, axis, pairs)


def genome_index(positions, genome_starts):
    inside = genome_starts[None, :] <= positions[:, None]
    return jnp.sum(inside.astype(jnp.int32), axis=1) - 1


def genome_begin(positions, genome_starts):
    inside = genome_starts[None, :] <= positions[:, None]
    return jnp.max(jnp.where(inside, genome_starts[None, :], 0), axis=1)


def grouped_filter(product, parity, filters, left_pad):
    channels = product.shape[1]
    group_width = channels // filters.shape[0]
    kernel = jnp.repeat(filters, group_width, axis=0).T[::-1][:, None, :]
    nothing = jnp.zeros_like(product)
    even_rows = jnp.where((parity == 0)[:, None], product, nothing)
    odd_rows = jnp.where((parity == 1)[:, None], product, nothing)
    stacked = jnp.stack([even_rows, odd_rows])
    return lax.conv_general_dilated(
        stacked,
        kernel,
        (1,),
        [(left_pad, 0)],
        dimension_numbers=("NWC", "WIO", "NWC"),
        feature_group_count=channels,
        preferred_element_type=jnp.float32,
    )


def attend_update(carried, queries, query_pos, query_begin, key_heads, value_heads, key_pos):
    weighted, running_max, weight_sum = carried
    score_scale = 1.0 / math.sqrt(HEAD_DIM)
    scores = (
        jnp.einsum("qhd,khd->hqk", queries, key_heads, preferred_element_type=jnp.float32)
        * score_scale
    )
    visible = (key_pos[None, :] <= query_pos[:, None]) & (key_pos[None, :] >= query_begin[:, None])
    new_max = jnp.maximum(running_max, jnp.max(jnp.where(visible[None], scores, -1e30), axis=2))
    weights = jnp.exp(jnp.where(visible[None], scores - new_max[:, :, None], -1e30))
    mixed = jnp.einsum(
        "hqk,khd->hqd",
        weights.astype(jnp.bfloat16),
        value_heads,
        preferred_element_type=jnp.float32,
    )
    return (mixed, new_max, jnp.sum(weights, axis=2))


def keep_state(carried):
    return carried


def gathered_plan(
    hyena_query, hyena_key, hyena_value, filters, skip_gain, attn_query, attn_key, genome_starts
):
    local_rows, channels = hyena_key.shape
    taps = filters.shape[1]
    shard_first = lax.axis_index("ctx") * local_rows
    product = lax.optimization_barrier(
        (hyena_key.astype(jnp.float32) * hyena_value.astype(jnp.float32)).astype(jnp.bfloat16)
    )
    earlier = passed_along(product[local_rows - (taps - 1) :], "ctx", 1)
    extended = jnp.concatenate([earlier, product], axis=0)
    extended_pos = shard_first - (taps - 1) + jnp.arange(local_rows + taps - 1, dtype=jnp.int32)
    both_parities = grouped_filter(
        extended, genome_index(extended_pos, genome_starts) % 2, filters, 0
    )
    own_pos = shard_first + jnp.arange(local_rows, dtype=jnp.int32)
    own_parity = genome_index(own_pos, genome_starts) % 2
    filtered = jnp.where((own_parity == 0)[:, None], both_parities[0], both_parities[1])
    hyena_mix = (
        hyena_query.astype(jnp.float32)
        * (filtered + skip_gain[None, :] * product.astype(jnp.float32))
    ).astype(jnp.bfloat16)
    head_count = channels // HEAD_DIM
    queries = attn_query.reshape(local_rows, head_count, HEAD_DIM)
    pairs = [(queries, own_pos)]
    groups = [
        (group_queries, group_pos, genome_begin(group_pos, genome_starts))
        for group_queries, group_pos in pairs
    ]
    initial = tuple(
        (
            (
                jnp.zeros((head_count, group_pos.shape[0], HEAD_DIM), jnp.float32),
                jnp.full((head_count, group_pos.shape[0]), -1e30, jnp.float32),
                jnp.zeros((head_count, group_pos.shape[0]), jnp.float32),
            )
            for group_queries, group_pos, group_begin in groups
        )
    )
    offset_row = jnp.int32(0)
    keys_piece = lax.all_gather(attn_key, "ctx", axis=0, tiled=True)
    values_piece = lax.all_gather(hyena_mix, "ctx", axis=0, tiled=True)
    key_rows = keys_piece.shape[0]
    key_heads = keys_piece.reshape(key_rows, head_count, HEAD_DIM)
    value_heads = values_piece.reshape(key_rows, head_count, HEAD_DIM)
    key_pos = jnp.arange(key_rows, dtype=jnp.int32)
    updated = []
    for state_now, (group_queries, group_pos, group_begin) in zip(initial, groups):
        needed = (offset_row <= jnp.max(group_pos)) & (offset_row + key_rows > jnp.min(group_begin))
        update = partial(
            attend_update,
            queries=group_queries,
            query_pos=group_pos,
            query_begin=group_begin,
            key_heads=key_heads,
            value_heads=value_heads,
            key_pos=key_pos,
        )
        updated.append(lax.cond(needed, update, keep_state, state_now))
    results = tuple(updated)
    outputs = []
    for weighted, running_max, weight_sum in results:
        finished = (weighted / weight_sum[:, :, None]).astype(jnp.bfloat16)
        outputs.append(finished.transpose(1, 0, 2).reshape(weighted.shape[1], channels))
    attended = outputs[0]
    return (hyena_mix, attended)


NEVER = -1e29
BLOCK = 128
CHUNKS = 4
AHEAD = 2
BACK = 2
EXPONENT = math.log2(math.e) / math.sqrt(HEAD_DIM)


def begin_of(positions, facts_ref, genomes):
    begin = jnp.zeros_like(positions)
    for genome in range(genomes):
        start = facts_ref[genome]
        begin = jnp.where(start <= positions, jnp.maximum(begin, start), begin)
    return begin


def hyena_kernel(genomes, facts_ref, query_ref, key_ref, value_ref, halo_ref, taps_ref, gain_ref,
                 mix_ref, extended, masks, bands):
    rows = key_ref.shape[0]
    blocks = rows // BLOCK
    groups = taps_ref.shape[0]
    group_width = BLOCK // groups

    @pl.when(pl.program_id(0) == 0)
    def _():
        first = facts_ref[genomes] * rows
        for b in range(blocks):
            i = lax.broadcasted_iota(jnp.int32, (BLOCK, 2 * BLOCK), 0)
            j = lax.broadcasted_iota(jnp.int32, (BLOCK, 2 * BLOCK), 1) - BLOCK
            begin = begin_of(i + (first + b * BLOCK), facts_ref, genomes)
            tap = i - j
            inside = (tap >= 0) & (tap < BLOCK) & (j + (first + b * BLOCK) >= begin)
            masks[b] = jnp.where(inside, 1.0, 0.0).astype(jnp.bfloat16)

    product = (key_ref[...].astype(jnp.float32) * value_ref[...].astype(jnp.float32)).astype(
        jnp.bfloat16
    )
    extended[:BLOCK] = halo_ref[...]
    extended[BLOCK:] = product
    lane_group = lax.broadcasted_iota(jnp.int32, (BLOCK, BLOCK), 1) // group_width
    for g in range(groups):
        row = jnp.broadcast_to(taps_ref[g : g + 1, :], (8, BLOCK))
        first = pltpu.roll(row, 0, 1, stride=1, stride_axis=0)
        turned = jnp.concatenate(
            [first] + [pltpu.roll(first, 8 * k, 1) for k in range(1, BLOCK // 8)]
        ).astype(jnp.bfloat16)
        both = jnp.concatenate([turned, turned], axis=1)
        for b in range(blocks):
            bands[b, g * BLOCK : (g + 1) * BLOCK] = both * masks[b]
    totals = []
    for b in range(blocks):
        parts = jnp.dot(
            bands[b], extended[b * BLOCK : (b + 2) * BLOCK], preferred_element_type=jnp.float32
        )
        picked = parts[:BLOCK]
        for g in range(1, groups):
            picked = jnp.where(lane_group == g, parts[g * BLOCK : (g + 1) * BLOCK], picked)
        totals.append(picked)
    for b in range(blocks):
        here = slice(b * BLOCK, (b + 1) * BLOCK)
        wide = extended[(b + 1) * BLOCK : (b + 2) * BLOCK].astype(jnp.float32)
        mix_ref[here] = (
            query_ref[here].astype(jnp.float32) * (totals[b] + gain_ref[...] * wide)
        ).astype(jnp.bfloat16)


def hyena(facts, genomes, query, key, value, halo, turned_taps, skip_gain):
    rows, channels = key.shape
    groups = turned_taps.shape[0] * BLOCK // channels
    column = lambda c, facts_ref: (0, c)
    return pl.pallas_call(
        partial(hyena_kernel, genomes),
        out_shape=jax.ShapeDtypeStruct((rows, channels), jnp.bfloat16),
        grid_spec=pltpu.PrefetchScalarGridSpec(
            num_scalar_prefetch=1,
            grid=(channels // BLOCK,),
            in_specs=[
                pl.BlockSpec((rows, BLOCK), column),
                pl.BlockSpec((rows, BLOCK), column),
                pl.BlockSpec((rows, BLOCK), column),
                pl.BlockSpec((BLOCK, BLOCK), column),
                pl.BlockSpec((groups, BLOCK), lambda c, facts_ref: (c, 0)),
                pl.BlockSpec((1, BLOCK), column),
            ],
            out_specs=pl.BlockSpec((rows, BLOCK), column),
            scratch_shapes=[
                pltpu.VMEM((rows + BLOCK, BLOCK), jnp.bfloat16),
                pltpu.VMEM((rows // BLOCK, BLOCK, 2 * BLOCK), jnp.bfloat16),
                pltpu.VMEM((rows // BLOCK, groups * BLOCK, 2 * BLOCK), jnp.bfloat16),
            ],
        ),
        cost_estimate=pl.CostEstimate(
            flops=rows * channels * 2 * 2 * BLOCK * groups,
            bytes_accessed=rows * channels * 8,
            transcendentals=0,
        ),
        name="hyena",
    )(facts, query, key, value, halo, turned_taps, skip_gain)


def attend_block(queries, keys, values, bias):
    scores = bias + lax.dot_general(
        queries, keys, (((1,), (1,)), ((), ())), preferred_element_type=jnp.float32
    )
    highest = jnp.maximum(jnp.max(scores, axis=1, keepdims=True), NEVER)
    weights = jnp.exp2((scores - highest) * EXPONENT).astype(jnp.bfloat16)
    mixed = jnp.dot(weights, values, preferred_element_type=jnp.float32)
    summed = mixed[:, HEAD_DIM:]
    some = summed > 0
    safe = jnp.where(some, summed, 1.0)
    log = jnp.where(some, highest * EXPONENT + jnp.log2(safe), NEVER)
    return mixed[:, :HEAD_DIM] / safe, log


def pieces_of(log):
    high = log.astype(jnp.bfloat16)
    rest = log - high.astype(jnp.float32)
    middle = rest.astype(jnp.bfloat16)
    low = (rest - middle.astype(jnp.float32)).astype(jnp.bfloat16)
    return jnp.concatenate([high, middle, low, jnp.zeros_like(low)])


def joined(pieces):
    wide = pieces.astype(jnp.float32)
    return wide[:8] + wide[8:16] + wide[16:24]


def attend_kernel(genomes, facts_ref, own_q, next_q, last_q, own_k, own_v, far_k, far_v,
                  own_o, next_o, last_o, own_l, queries, keys, values, bias, mixed, logs):
    rows, width = own_q.shape
    heads = width // HEAD_DIM
    per_shard = rows // BLOCK
    shard = facts_ref[genomes]
    own_first = shard * rows
    base = own_first - rows
    limit = jnp.where(shard == 1, base, own_first)
    steps = per_shard * jnp.where(shard == 1, 3, jnp.where(shard == 2, 2, 1))

    def rows_of(step):
        return pl.ds(pl.multiple_of(step * BLOCK, BLOCK), BLOCK)

    logs[...] = jnp.full_like(logs, NEVER)

    def fill(step, nothing):
        query_pos = own_first + step * BLOCK + lax.broadcasted_iota(jnp.int32, (BLOCK, 1), 0)
        begin = jnp.maximum(begin_of(query_pos, facts_ref, genomes), limit)
        key_pos = base + lax.broadcasted_iota(jnp.int32, (BLOCK, 2 * rows), 1)
        visible = (key_pos >= begin) & (key_pos <= query_pos)
        bias[rows_of(step), :] = jnp.where(visible, 0.0, 10 * NEVER)
        return nothing

    lax.fori_loop(0, steps, fill, 0)
    for slot, ref in enumerate((own_q, next_q, last_q)):
        queries[slot * rows : (slot + 1) * rows] = ref[...]
    for slot, (k_ref, v_ref) in enumerate(((far_k, far_v), (own_k, own_v))):
        here = slice(slot * rows, (slot + 1) * rows)
        keys[here] = k_ref[...]
        for head in range(heads):
            first = 2 * head * HEAD_DIM
            values[here, first : first + HEAD_DIM] = v_ref[:, head * HEAD_DIM : (head + 1) * HEAD_DIM]
            values[here, first + HEAD_DIM : first + 2 * HEAD_DIM] = jnp.ones(
                (rows, HEAD_DIM), jnp.bfloat16
            )

    def one_step(step, nothing):
        query_first = own_first + step * BLOCK
        begin = limit
        for genome in range(genomes):
            start = facts_ref[genome]
            begin = jnp.where(start <= query_first, jnp.maximum(begin, start), begin)
        first = (begin - base) // BLOCK
        last = jnp.minimum(query_first + BLOCK, own_first + rows)
        count = (last - base) // BLOCK - first

        @pl.when(count <= 0)
        def _():
            mixed[rows_of(step), :] = jnp.zeros((BLOCK, width), jnp.float32)

        for blocks in range(1, 2 * per_shard + 1):

            @pl.when(count == blocks)
            def _():
                span = pl.ds(pl.multiple_of(first * BLOCK, BLOCK), blocks * BLOCK)
                mask = bias[rows_of(step), span]
                lane = lax.broadcasted_iota(jnp.int32, (BLOCK, BLOCK), 1)
                gathered = jnp.full((BLOCK, BLOCK), NEVER, jnp.float32)
                for head in range(heads):
                    here = slice(head * HEAD_DIM, (head + 1) * HEAD_DIM)
                    both = slice(2 * head * HEAD_DIM, 2 * (head + 1) * HEAD_DIM)
                    out, log = attend_block(
                        queries[rows_of(step), here], keys[span, here], values[span, both], mask
                    )
                    mixed[rows_of(step), here] = out
                    gathered = jnp.where(lane == head, log, gathered)
                logs[rows_of(step), :] = gathered

        return nothing

    lax.fori_loop(0, steps, one_step, 0)
    own_o[...] = mixed[:rows].astype(own_o.dtype)
    own_l[...] = jnp.transpose(logs[:rows])[:8]
    for slot, ref, used in ((1, next_o, (shard == 1) | (shard == 2)), (2, last_o, shard == 1)):

        @pl.when(used)
        def _():
            here = slice(slot * rows, (slot + 1) * rows)
            ref[:rows] = mixed[here].astype(ref.dtype)
            ref[rows:, :rows] = pieces_of(jnp.transpose(logs[here])[:8])
            ref[rows:, rows:] = jnp.zeros((32, width - rows), ref.dtype)

        @pl.when(jnp.logical_not(used))
        def _():
            ref[...] = jnp.zeros_like(ref)


def attend(facts, genomes, chunk, heads, own_q, next_q, last_q, own_k, own_v, far_k, far_v):
    rows = own_q.shape[0]
    width = heads * HEAD_DIM
    whole = pl.BlockSpec((rows, width), lambda h, facts_ref: (0, chunk))
    piece = pl.BlockSpec((rows, width), lambda h, facts_ref: (0, 0))
    halved = pl.BlockSpec((rows, width), lambda h, facts_ref: (0, chunk % (CHUNKS // 2)))
    sent = pl.BlockSpec((rows + 32, width), lambda h, facts_ref: (0, 0))
    logs = pl.BlockSpec((8, rows), lambda h, facts_ref: (0, 0))
    return pl.pallas_call(
        partial(attend_kernel, genomes),
        out_shape=(
            jax.ShapeDtypeStruct((rows, width), jnp.bfloat16),
            jax.ShapeDtypeStruct((rows + 32, width), jnp.bfloat16),
            jax.ShapeDtypeStruct((rows + 32, width), jnp.bfloat16),
            jax.ShapeDtypeStruct((8, rows), jnp.float32),
        ),
        grid_spec=pltpu.PrefetchScalarGridSpec(
            num_scalar_prefetch=1,
            grid=(1,),
            in_specs=[whole, halved, halved, whole, whole, whole, piece],
            out_specs=[piece, sent, sent, logs],
            scratch_shapes=[
                pltpu.VMEM((3 * rows, width), jnp.bfloat16),
                pltpu.VMEM((2 * rows, width), jnp.bfloat16),
                pltpu.VMEM((2 * rows, 2 * width), jnp.bfloat16),
                pltpu.VMEM((3 * rows, 2 * rows), jnp.float32),
                pltpu.VMEM((3 * rows, width), jnp.float32),
                pltpu.VMEM((3 * rows, BLOCK), jnp.float32),
            ],
        ),
        compiler_params=pltpu.CompilerParams(vmem_limit_bytes=32 << 20),
        cost_estimate=pl.CostEstimate(
            flops=12 * rows * rows * width,
            bytes_accessed=rows * width * 22,
            transcendentals=3 * rows * rows * heads,
        ),
        name="attend",
    )(facts, own_q, next_q, last_q, own_k, own_v, far_k, far_v)


def combine_kernel(genomes, heads, facts_ref, *refs):
    out_ref = refs[-1]
    width = heads * HEAD_DIM
    shard = facts_ref[genomes]
    for chunk in range(CHUNKS):
        own_o, near_o, far_o, own_l, near_l, far_l = refs[6 * chunk : 6 * chunk + 6]
        own = own_l[...]
        near = jnp.where(shard >= 2, joined(near_l[...]), NEVER)
        far = jnp.where(shard == 3, joined(far_l[...]), NEVER)
        highest = jnp.maximum(own, jnp.maximum(near, far))
        shares = [jnp.exp2(log - highest) for log in (own, near, far)]
        whole = shares[0] + shares[1] + shares[2]
        columns = [
            jnp.transpose(
                jnp.concatenate([share / whole, jnp.zeros((BLOCK - 8, BLOCK), jnp.float32)])
            )
            for share in shares
        ]
        for head in range(heads):
            here = slice(head * HEAD_DIM, (head + 1) * HEAD_DIM)
            mixed = columns[0][:, head : head + 1] * own_o[:, here].astype(jnp.float32)
            for column, ref in ((columns[1], near_o), (columns[2], far_o)):
                mixed += column[:, head : head + 1] * ref[:, here].astype(jnp.float32)
            first = chunk * width + head * HEAD_DIM
            out_ref[:, first : first + HEAD_DIM] = mixed.astype(out_ref.dtype)


def combine(facts, genomes, heads, channels, parts):
    rows, width = parts[0][0].shape
    piece = pl.BlockSpec((BLOCK, width), lambda r, facts_ref: (r, 0))
    own = pl.BlockSpec((8, BLOCK), lambda r, facts_ref: (0, r))
    logs = pl.BlockSpec((32, BLOCK), lambda r, facts_ref: (rows // 32, r))
    operands = [x for o, near, far, l in parts for x in (o, near, far, l, near, far)]
    return pl.pallas_call(
        partial(combine_kernel, genomes, heads),
        out_shape=jax.ShapeDtypeStruct((rows, channels), jnp.bfloat16),
        grid_spec=pltpu.PrefetchScalarGridSpec(
            num_scalar_prefetch=1,
            grid=(rows // BLOCK,),
            in_specs=[piece, piece, piece, own, logs, logs] * CHUNKS,
            out_specs=pl.BlockSpec((BLOCK, channels), lambda r, facts_ref: (r, 0)),
        ),
        cost_estimate=pl.CostEstimate(
            flops=rows * channels * 16, bytes_accessed=rows * channels * 10, transcendentals=0
        ),
        name="combine",
    )(facts, *operands)


def balanced_plan(
    hyena_query, hyena_key, hyena_value, filters, skip_gain, attn_query, attn_key, genome_starts
):
    rows, channels = hyena_key.shape
    genomes = genome_starts.shape[0]
    shard = lax.axis_index("ctx")
    facts = jnp.concatenate([genome_starts, jnp.full((1,), shard, jnp.int32)])
    tail = (
        hyena_key[rows - BLOCK :].astype(jnp.float32)
        * hyena_value[rows - BLOCK :].astype(jnp.float32)
    ).astype(jnp.bfloat16)
    halo = passed_along(tail, "ctx", 1)
    far_k = lax.ppermute(attn_key, "ctx", [(0, 1)])
    first_queries = attn_query[:, : channels // 2]
    turned_taps = jnp.roll(filters[:, ::-1], 1, axis=1).astype(jnp.float32)
    mix = hyena(
        facts, genomes, hyena_query, hyena_key, hyena_value, halo, turned_taps, skip_gain[None, :]
    )
    heads = channels // HEAD_DIM // CHUNKS
    width = heads * HEAD_DIM
    half = channels // 2
    later_queries, mix = lax.optimization_barrier((attn_query[:, half:], mix))
    next_qs, last_qs = [], []
    for queries in (first_queries, later_queries):
        next_qs.append(lax.ppermute(queries, "ctx", [(2, 1), (3, 2)]))
        last_qs.append(lax.ppermute(queries, "ctx", [(3, 1)]))
    parts = []
    for chunk in range(CHUNKS):
        sent_v = mix[:, chunk * width : (chunk + 1) * width]
        if chunk >= AHEAD:
            own_o = parts[chunk - AHEAD][0]
            sent_v, own_o = lax.optimization_barrier((sent_v, own_o))
            parts[chunk - AHEAD] = (own_o,) + parts[chunk - AHEAD][1:]
        far_v = lax.ppermute(sent_v, "ctx", [(0, 1)])
        if chunk >= BACK:
            far_v, parts[chunk - BACK] = lax.optimization_barrier((far_v, parts[chunk - BACK]))
        part = 2 * chunk // CHUNKS
        own_o, next_o, last_o, own_l = attend(
            facts, genomes, chunk, heads, attn_query, next_qs[part], last_qs[part], attn_key, mix,
            far_k, far_v,
        )
        parts.append(
            (
                own_o,
                lax.ppermute(next_o, "ctx", [(1, 2), (2, 3)]),
                lax.ppermute(last_o, "ctx", [(1, 3)]),
                own_l,
            )
        )
    return (mix, combine(facts, genomes, heads, channels, parts))


def solution(mesh):
    return jax.shard_map(
        balanced_plan if mesh.shape["ctx"] == 4 else gathered_plan,
        mesh=mesh,
        in_specs=(
            P(("rep", "ctx"), ("ch", "sub")),
            P(("rep", "ctx"), ("ch", "sub")),
            P(("rep", "ctx"), ("ch", "sub")),
            P(("ch", "sub"), None),
            P(("ch", "sub")),
            P(("rep", "ctx"), ("ch", "sub")),
            P(("rep", "ctx"), ("ch", "sub")),
            P("rep"),
        ),
        out_specs=(P(("rep", "ctx"), ("ch", "sub")), P(("rep", "ctx"), ("ch", "sub"))),
        check_vma=False,
    )
```

```python
from functools import partial
import math

import jax
import jax.numpy as jnp
from jax import lax
from jax.experimental import pallas as pl
from jax.experimental.pallas import tpu as pltpu
from jax.sharding import PartitionSpec as P

HEAD_DIM = 128


def passed_along(value, axis, by):
    devices = lax.axis_size(axis)
    pairs = [(i, i + by) for i in range(devices) if 0 <= i + by < devices]
    return lax.ppermute(value, axis, pairs)


def genome_index(positions, genome_starts):
    inside = genome_starts[None, :] <= positions[:, None]
    return jnp.sum(inside.astype(jnp.int32), axis=1) - 1


def genome_begin(positions, genome_starts):
    inside = genome_starts[None, :] <= positions[:, None]
    return jnp.max(jnp.where(inside, genome_starts[None, :], 0), axis=1)


def grouped_filter(product, parity, filters, left_pad):
    channels = product.shape[1]
    group_width = channels // filters.shape[0]
    kernel = jnp.repeat(filters, group_width, axis=0).T[::-1][:, None, :]
    nothing = jnp.zeros_like(product)
    even_rows = jnp.where((parity == 0)[:, None], product, nothing)
    odd_rows = jnp.where((parity == 1)[:, None], product, nothing)
    stacked = jnp.stack([even_rows, odd_rows])
    return lax.conv_general_dilated(
        stacked,
        kernel,
        (1,),
        [(left_pad, 0)],
        dimension_numbers=("NWC", "WIO", "NWC"),
        feature_group_count=channels,
        preferred_element_type=jnp.float32,
    )


def attend_update(carried, queries, query_pos, query_begin, key_heads, value_heads, key_pos):
    weighted, running_max, weight_sum = carried
    score_scale = 1.0 / math.sqrt(HEAD_DIM)
    scores = (
        jnp.einsum("qhd,khd->hqk", queries, key_heads, preferred_element_type=jnp.float32)
        * score_scale
    )
    visible = (key_pos[None, :] <= query_pos[:, None]) & (key_pos[None, :] >= query_begin[:, None])
    new_max = jnp.maximum(running_max, jnp.max(jnp.where(visible[None], scores, -1e30), axis=2))
    weights = jnp.exp(jnp.where(visible[None], scores - new_max[:, :, None], -1e30))
    mixed = jnp.einsum(
        "hqk,khd->hqd",
        weights.astype(jnp.bfloat16),
        value_heads,
        preferred_element_type=jnp.float32,
    )
    return (mixed, new_max, jnp.sum(weights, axis=2))


def keep_state(carried):
    return carried


def gathered_plan(
    hyena_query, hyena_key, hyena_value, filters, skip_gain, attn_query, attn_key, genome_starts
):
    local_rows, channels = hyena_key.shape
    taps = filters.shape[1]
    shard_first = lax.axis_index("ctx") * local_rows
    product = lax.optimization_barrier(
        (hyena_key.astype(jnp.float32) * hyena_value.astype(jnp.float32)).astype(jnp.bfloat16)
    )
    earlier = passed_along(product[local_rows - (taps - 1) :], "ctx", 1)
    extended = jnp.concatenate([earlier, product], axis=0)
    extended_pos = shard_first - (taps - 1) + jnp.arange(local_rows + taps - 1, dtype=jnp.int32)
    both_parities = grouped_filter(
        extended, genome_index(extended_pos, genome_starts) % 2, filters, 0
    )
    own_pos = shard_first + jnp.arange(local_rows, dtype=jnp.int32)
    own_parity = genome_index(own_pos, genome_starts) % 2
    filtered = jnp.where((own_parity == 0)[:, None], both_parities[0], both_parities[1])
    hyena_mix = (
        hyena_query.astype(jnp.float32)
        * (filtered + skip_gain[None, :] * product.astype(jnp.float32))
    ).astype(jnp.bfloat16)
    head_count = channels // HEAD_DIM
    queries = attn_query.reshape(local_rows, head_count, HEAD_DIM)
    pairs = [(queries, own_pos)]
    groups = [
        (group_queries, group_pos, genome_begin(group_pos, genome_starts))
        for group_queries, group_pos in pairs
    ]
    initial = tuple(
        (
            (
                jnp.zeros((head_count, group_pos.shape[0], HEAD_DIM), jnp.float32),
                jnp.full((head_count, group_pos.shape[0]), -1e30, jnp.float32),
                jnp.zeros((head_count, group_pos.shape[0]), jnp.float32),
            )
            for group_queries, group_pos, group_begin in groups
        )
    )
    offset_row = jnp.int32(0)
    keys_piece = lax.all_gather(attn_key, "ctx", axis=0, tiled=True)
    values_piece = lax.all_gather(hyena_mix, "ctx", axis=0, tiled=True)
    key_rows = keys_piece.shape[0]
    key_heads = keys_piece.reshape(key_rows, head_count, HEAD_DIM)
    value_heads = values_piece.reshape(key_rows, head_count, HEAD_DIM)
    key_pos = jnp.arange(key_rows, dtype=jnp.int32)
    updated = []
    for state_now, (group_queries, group_pos, group_begin) in zip(initial, groups):
        needed = (offset_row <= jnp.max(group_pos)) & (offset_row + key_rows > jnp.min(group_begin))
        update = partial(
            attend_update,
            queries=group_queries,
            query_pos=group_pos,
            query_begin=group_begin,
            key_heads=key_heads,
            value_heads=value_heads,
            key_pos=key_pos,
        )
        updated.append(lax.cond(needed, update, keep_state, state_now))
    results = tuple(updated)
    outputs = []
    for weighted, running_max, weight_sum in results:
        finished = (weighted / weight_sum[:, :, None]).astype(jnp.bfloat16)
        outputs.append(finished.transpose(1, 0, 2).reshape(weighted.shape[1], channels))
    attended = outputs[0]
    return (hyena_mix, attended)


NEVER = -1e29
BLOCK = 128
CHUNKS = 4
AHEAD = 2
BACK = 2
EXPONENT = math.log2(math.e) / math.sqrt(HEAD_DIM)


def begin_of(positions, facts_ref, genomes):
    begin = jnp.zeros_like(positions)
    for genome in range(genomes):
        start = facts_ref[genome]
        begin = jnp.where(start <= positions, jnp.maximum(begin, start), begin)
    return begin


def hyena_kernel(genomes, facts_ref, query_ref, key_ref, value_ref, halo_ref, taps_ref, gain_ref,
                 mix_ref, extended, masks, bands):
    rows = key_ref.shape[0]
    blocks = rows // BLOCK
    groups = taps_ref.shape[0] * BLOCK // key_ref.shape[1]
    group_width = BLOCK // groups

    @pl.when(pl.program_id(0) == 0)
    def _():
        first = facts_ref[genomes] * rows
        for b in range(blocks):
            i = lax.broadcasted_iota(jnp.int32, (BLOCK, 2 * BLOCK), 0)
            j = lax.broadcasted_iota(jnp.int32, (BLOCK, 2 * BLOCK), 1) - BLOCK
            begin = begin_of(i + (first + b * BLOCK), facts_ref, genomes)
            tap = i - j
            inside = (tap >= 0) & (tap < BLOCK) & (j + (first + b * BLOCK) >= begin)
            masks[b] = jnp.where(inside, 1.0, 0.0).astype(jnp.bfloat16)

    lane_group = lax.broadcasted_iota(jnp.int32, (BLOCK, BLOCK), 1) // group_width

    def one_tile(tile, nothing):
        lanes = pl.ds(pl.multiple_of(tile * BLOCK, BLOCK), BLOCK)
        product = key_ref[:, lanes].astype(jnp.float32) * value_ref[:, lanes].astype(jnp.float32)
        extended[:BLOCK] = halo_ref[:, lanes]
        extended[BLOCK:] = product.astype(jnp.bfloat16)
        for g in range(groups):
            row = jnp.broadcast_to(taps_ref[pl.ds(tile * groups + g, 1), :], (8, BLOCK))
            first = pltpu.roll(row, 0, 1, stride=1, stride_axis=0)
            turned = jnp.concatenate(
                [first] + [pltpu.roll(first, 8 * k, 1) for k in range(1, BLOCK // 8)]
            ).astype(jnp.bfloat16)
            both = jnp.concatenate([turned, turned], axis=1)
            for b in range(blocks):
                bands[b, g * BLOCK : (g + 1) * BLOCK] = both * masks[b]
        for b in range(blocks):
            parts = jnp.dot(
                bands[b], extended[b * BLOCK : (b + 2) * BLOCK], preferred_element_type=jnp.float32
            )
            total = parts[:BLOCK]
            for g in range(1, groups):
                total = jnp.where(lane_group == g, parts[g * BLOCK : (g + 1) * BLOCK], total)
            here = slice(b * BLOCK, (b + 1) * BLOCK)
            wide = extended[(b + 1) * BLOCK : (b + 2) * BLOCK].astype(jnp.float32)
            mix_ref[here, lanes] = (
                query_ref[here, lanes].astype(jnp.float32) * (total + gain_ref[:, lanes] * wide)
            ).astype(jnp.bfloat16)
        return nothing

    lax.fori_loop(0, key_ref.shape[1] // BLOCK, one_tile, 0)


def hyena(facts, genomes, query, key, value, halo, turned_taps, skip_gain):
    rows, channels = key.shape
    groups = turned_taps.shape[0] * BLOCK // channels
    wide = 4 * BLOCK
    column = lambda c, facts_ref: (0, c)
    return pl.pallas_call(
        partial(hyena_kernel, genomes),
        out_shape=jax.ShapeDtypeStruct((rows, channels), jnp.bfloat16),
        grid_spec=pltpu.PrefetchScalarGridSpec(
            num_scalar_prefetch=1,
            grid=(channels // wide,),
            in_specs=[
                pl.BlockSpec((rows, wide), column),
                pl.BlockSpec((rows, wide), column),
                pl.BlockSpec((rows, wide), column),
                pl.BlockSpec((BLOCK, wide), column),
                pl.BlockSpec((groups * wide // BLOCK, BLOCK), lambda c, facts_ref: (c, 0)),
                pl.BlockSpec((1, wide), column),
            ],
            out_specs=pl.BlockSpec((rows, wide), column),
            scratch_shapes=[
                pltpu.VMEM((rows + BLOCK, BLOCK), jnp.bfloat16),
                pltpu.VMEM((rows // BLOCK, BLOCK, 2 * BLOCK), jnp.bfloat16),
                pltpu.VMEM((rows // BLOCK, groups * BLOCK, 2 * BLOCK), jnp.bfloat16),
            ],
        ),
        compiler_params=pltpu.CompilerParams(vmem_limit_bytes=32 << 20),
        cost_estimate=pl.CostEstimate(
            flops=rows * channels * 2 * 2 * BLOCK * groups,
            bytes_accessed=rows * channels * 8,
            transcendentals=0,
        ),
        name="hyena",
    )(facts, query, key, value, halo, turned_taps, skip_gain)


def attend_block(queries, keys, values, bias):
    scores = bias + lax.dot_general(
        queries, keys, (((1,), (1,)), ((), ())), preferred_element_type=jnp.float32
    )
    highest = jnp.maximum(jnp.max(scores, axis=1, keepdims=True), NEVER)
    weights = jnp.exp2((scores - highest) * EXPONENT).astype(jnp.bfloat16)
    mixed = jnp.dot(weights, values, preferred_element_type=jnp.float32)
    summed = mixed[:, HEAD_DIM:]
    some = summed > 0
    safe = jnp.where(some, summed, 1.0)
    log = jnp.where(some, highest * EXPONENT + jnp.log2(safe), NEVER)
    return mixed[:, :HEAD_DIM] / safe, log


def pieces_of(log):
    high = log.astype(jnp.bfloat16)
    rest = log - high.astype(jnp.float32)
    middle = rest.astype(jnp.bfloat16)
    low = (rest - middle.astype(jnp.float32)).astype(jnp.bfloat16)
    return jnp.concatenate([high, middle, low, jnp.zeros_like(low)])


def joined(pieces):
    wide = pieces.astype(jnp.float32)
    return wide[:8] + wide[8:16] + wide[16:24]


def attend_kernel(genomes, facts_ref, own_q, next_q, last_q, own_k, own_v, far_k, far_v,
                  own_o, next_o, last_o, own_l, queries, keys, values, bias, mixed, logs):
    rows, width = own_q.shape
    heads = width // HEAD_DIM
    per_shard = rows // BLOCK
    shard = facts_ref[genomes]
    own_first = shard * rows
    base = own_first - rows
    limit = jnp.where(shard == 1, base, own_first)
    steps = per_shard * jnp.where(shard == 1, 3, jnp.where(shard == 2, 2, 1))

    def rows_of(step):
        return pl.ds(pl.multiple_of(step * BLOCK, BLOCK), BLOCK)

    logs[...] = jnp.full_like(logs, NEVER)

    def fill(step, nothing):
        query_pos = own_first + step * BLOCK + lax.broadcasted_iota(jnp.int32, (BLOCK, 1), 0)
        begin = jnp.maximum(begin_of(query_pos, facts_ref, genomes), limit)
        key_pos = base + lax.broadcasted_iota(jnp.int32, (BLOCK, 2 * rows), 1)
        visible = (key_pos >= begin) & (key_pos <= query_pos)
        bias[rows_of(step), :] = jnp.where(visible, 0.0, 10 * NEVER)
        return nothing

    lax.fori_loop(0, steps, fill, 0)
    for slot, ref in enumerate((own_q, next_q, last_q)):
        queries[slot * rows : (slot + 1) * rows] = ref[...]
    for slot, (k_ref, v_ref) in enumerate(((far_k, far_v), (own_k, own_v))):
        here = slice(slot * rows, (slot + 1) * rows)
        keys[here] = k_ref[...]
        for head in range(heads):
            first = 2 * head * HEAD_DIM
            values[here, first : first + HEAD_DIM] = v_ref[:, head * HEAD_DIM : (head + 1) * HEAD_DIM]
            values[here, first + HEAD_DIM : first + 2 * HEAD_DIM] = jnp.ones(
                (rows, HEAD_DIM), jnp.bfloat16
            )

    def one_step(step, nothing):
        query_first = own_first + step * BLOCK
        begin = limit
        for genome in range(genomes):
            start = facts_ref[genome]
            begin = jnp.where(start <= query_first, jnp.maximum(begin, start), begin)
        first = (begin - base) // BLOCK
        last = jnp.minimum(query_first + BLOCK, own_first + rows)
        count = (last - base) // BLOCK - first

        @pl.when(count <= 0)
        def _():
            mixed[rows_of(step), :] = jnp.zeros((BLOCK, width), jnp.float32)

        for blocks in range(1, 2 * per_shard + 1):

            @pl.when(count == blocks)
            def _():
                span = pl.ds(pl.multiple_of(first * BLOCK, BLOCK), blocks * BLOCK)
                mask = bias[rows_of(step), span]
                lane = lax.broadcasted_iota(jnp.int32, (BLOCK, BLOCK), 1)
                gathered = jnp.full((BLOCK, BLOCK), NEVER, jnp.float32)
                for head in range(heads):
                    here = slice(head * HEAD_DIM, (head + 1) * HEAD_DIM)
                    both = slice(2 * head * HEAD_DIM, 2 * (head + 1) * HEAD_DIM)
                    out, log = attend_block(
                        queries[rows_of(step), here], keys[span, here], values[span, both], mask
                    )
                    mixed[rows_of(step), here] = out
                    gathered = jnp.where(lane == head, log, gathered)
                logs[rows_of(step), :] = gathered

        return nothing

    lax.fori_loop(0, steps, one_step, 0)
    own_o[...] = mixed[:rows].astype(own_o.dtype)
    own_l[...] = jnp.transpose(logs[:rows])[:8]
    for slot, ref, used in ((1, next_o, (shard == 1) | (shard == 2)), (2, last_o, shard == 1)):

        @pl.when(used)
        def _():
            here = slice(slot * rows, (slot + 1) * rows)
            ref[:rows] = mixed[here].astype(ref.dtype)
            ref[rows:, :rows] = pieces_of(jnp.transpose(logs[here])[:8])
            ref[rows:, rows:] = jnp.zeros((32, width - rows), ref.dtype)

        @pl.when(jnp.logical_not(used))
        def _():
            ref[...] = jnp.zeros_like(ref)


def attend(facts, genomes, chunk, heads, own_q, next_q, last_q, own_k, own_v, far_k, far_v):
    rows = own_q.shape[0]
    width = heads * HEAD_DIM
    whole = pl.BlockSpec((rows, width), lambda h, facts_ref: (0, chunk))
    piece = pl.BlockSpec((rows, width), lambda h, facts_ref: (0, 0))
    halved = pl.BlockSpec((rows, width), lambda h, facts_ref: (0, chunk % (CHUNKS // 2)))
    sent = pl.BlockSpec((rows + 32, width), lambda h, facts_ref: (0, 0))
    logs = pl.BlockSpec((8, rows), lambda h, facts_ref: (0, 0))
    return pl.pallas_call(
        partial(attend_kernel, genomes),
        out_shape=(
            jax.ShapeDtypeStruct((rows, width), jnp.bfloat16),
            jax.ShapeDtypeStruct((rows + 32, width), jnp.bfloat16),
            jax.ShapeDtypeStruct((rows + 32, width), jnp.bfloat16),
            jax.ShapeDtypeStruct((8, rows), jnp.float32),
        ),
        grid_spec=pltpu.PrefetchScalarGridSpec(
            num_scalar_prefetch=1,
            grid=(1,),
            in_specs=[whole, halved, halved, whole, whole, whole, piece],
            out_specs=[piece, sent, sent, logs],
            scratch_shapes=[
                pltpu.VMEM((3 * rows, width), jnp.bfloat16),
                pltpu.VMEM((2 * rows, width), jnp.bfloat16),
                pltpu.VMEM((2 * rows, 2 * width), jnp.bfloat16),
                pltpu.VMEM((3 * rows, 2 * rows), jnp.float32),
                pltpu.VMEM((3 * rows, width), jnp.float32),
                pltpu.VMEM((3 * rows, BLOCK), jnp.float32),
            ],
        ),
        compiler_params=pltpu.CompilerParams(vmem_limit_bytes=32 << 20),
        cost_estimate=pl.CostEstimate(
            flops=12 * rows * rows * width,
            bytes_accessed=rows * width * 22,
            transcendentals=3 * rows * rows * heads,
        ),
        name="attend",
    )(facts, own_q, next_q, last_q, own_k, own_v, far_k, far_v)


def combine_kernel(genomes, heads, facts_ref, *refs):
    out_ref = refs[-1]
    width = heads * HEAD_DIM
    shard = facts_ref[genomes]
    for chunk in range(CHUNKS):
        own_o, near_o, far_o, own_l, near_l, far_l = refs[6 * chunk : 6 * chunk + 6]
        own = own_l[...]
        near = jnp.where(shard >= 2, joined(near_l[...]), NEVER)
        far = jnp.where(shard == 3, joined(far_l[...]), NEVER)
        highest = jnp.maximum(own, jnp.maximum(near, far))
        shares = [jnp.exp2(log - highest) for log in (own, near, far)]
        whole = shares[0] + shares[1] + shares[2]
        columns = [
            jnp.transpose(
                jnp.concatenate([share / whole, jnp.zeros((BLOCK - 8, BLOCK), jnp.float32)])
            )
            for share in shares
        ]
        for head in range(heads):
            here = slice(head * HEAD_DIM, (head + 1) * HEAD_DIM)
            mixed = columns[0][:, head : head + 1] * own_o[:, here].astype(jnp.float32)
            for column, ref in ((columns[1], near_o), (columns[2], far_o)):
                mixed += column[:, head : head + 1] * ref[:, here].astype(jnp.float32)
            first = chunk * width + head * HEAD_DIM
            out_ref[:, first : first + HEAD_DIM] = mixed.astype(out_ref.dtype)


def combine(facts, genomes, heads, channels, parts):
    rows, width = parts[0][0].shape
    piece = pl.BlockSpec((BLOCK, width), lambda r, facts_ref: (r, 0))
    own = pl.BlockSpec((8, BLOCK), lambda r, facts_ref: (0, r))
    logs = pl.BlockSpec((32, BLOCK), lambda r, facts_ref: (rows // 32, r))
    operands = [x for o, near, far, l in parts for x in (o, near, far, l, near, far)]
    return pl.pallas_call(
        partial(combine_kernel, genomes, heads),
        out_shape=jax.ShapeDtypeStruct((rows, channels), jnp.bfloat16),
        grid_spec=pltpu.PrefetchScalarGridSpec(
            num_scalar_prefetch=1,
            grid=(rows // BLOCK,),
            in_specs=[piece, piece, piece, own, logs, logs] * CHUNKS,
            out_specs=pl.BlockSpec((BLOCK, channels), lambda r, facts_ref: (r, 0)),
        ),
        cost_estimate=pl.CostEstimate(
            flops=rows * channels * 16, bytes_accessed=rows * channels * 10, transcendentals=0
        ),
        name="combine",
    )(facts, *operands)


def balanced_plan(
    hyena_query, hyena_key, hyena_value, filters, skip_gain, attn_query, attn_key, genome_starts
):
    rows, channels = hyena_key.shape
    genomes = genome_starts.shape[0]
    shard = lax.axis_index("ctx")
    facts = jnp.concatenate([genome_starts, jnp.full((1,), shard, jnp.int32)])
    tail = (
        hyena_key[rows - BLOCK :].astype(jnp.float32)
        * hyena_value[rows - BLOCK :].astype(jnp.float32)
    ).astype(jnp.bfloat16)
    halo = passed_along(tail, "ctx", 1)
    sent_k, halo = lax.optimization_barrier((attn_key, halo))
    far_k = lax.ppermute(sent_k, "ctx", [(0, 1)])
    first_queries = attn_query[:, : channels // 2]
    turned_taps = jnp.roll(filters[:, ::-1], 1, axis=1).astype(jnp.float32)
    mix = hyena(
        facts, genomes, hyena_query, hyena_key, hyena_value, halo, turned_taps, skip_gain[None, :]
    )
    heads = channels // HEAD_DIM // CHUNKS
    width = heads * HEAD_DIM
    half = channels // 2
    later_queries, mix = lax.optimization_barrier((attn_query[:, half:], mix))
    next_qs, last_qs = [], []
    for queries in (first_queries, later_queries):
        next_qs.append(lax.ppermute(queries, "ctx", [(2, 1), (3, 2)]))
        last_qs.append(lax.ppermute(queries, "ctx", [(3, 1)]))
    parts = []
    for chunk in range(CHUNKS):
        sent_v = mix[:, chunk * width : (chunk + 1) * width]
        if chunk >= AHEAD:
            own_o = parts[chunk - AHEAD][0]
            sent_v, own_o = lax.optimization_barrier((sent_v, own_o))
            parts[chunk - AHEAD] = (own_o,) + parts[chunk - AHEAD][1:]
        far_v = lax.ppermute(sent_v, "ctx", [(0, 1)])
        if chunk >= BACK:
            far_v, parts[chunk - BACK] = lax.optimization_barrier((far_v, parts[chunk - BACK]))
        part = 2 * chunk // CHUNKS
        own_o, next_o, last_o, own_l = attend(
            facts, genomes, chunk, heads, attn_query, next_qs[part], last_qs[part], attn_key, mix,
            far_k, far_v,
        )
        parts.append(
            (
                own_o,
                lax.ppermute(next_o, "ctx", [(1, 2), (2, 3)]),
                lax.ppermute(last_o, "ctx", [(1, 3)]),
                own_l,
            )
        )
    return (mix, combine(facts, genomes, heads, channels, parts))


def solution(mesh):
    return jax.shard_map(
        balanced_plan if mesh.shape["ctx"] == 4 else gathered_plan,
        mesh=mesh,
        in_specs=(
            P(("rep", "ctx"), ("ch", "sub")),
            P(("rep", "ctx"), ("ch", "sub")),
            P(("rep", "ctx"), ("ch", "sub")),
            P(("ch", "sub"), None),
            P(("ch", "sub")),
            P(("rep", "ctx"), ("ch", "sub")),
            P(("rep", "ctx"), ("ch", "sub")),
            P("rep"),
        ),
        out_specs=(P(("rep", "ctx"), ("ch", "sub")), P(("rep", "ctx"), ("ch", "sub"))),
        check_vma=False,
    )
```
